32 devices in a mesh: energy: 8 (over z, core), block: 4 (over y, x).
Axes of the slice: x: 2, y: 2, z: 4, core: 2. Of those that a mesh axis runs over, the one named last changes fastest.
Arguments:
- g_lesser: float32 [2, 8, 1024, 256], P(None, 'energy', 'block'), may hold values from -0.75 to 0.75
- g_greater: float32 [2, 8, 1024, 256], P(None, 'energy', 'block'), may hold values from -0.75 to 0.75
- onsite: float32 [2, 8, 1024, 256], P(None, 'energy', 'block'), may hold values from -1 to 7
- lower: float32 [2, 1024, 256], P(None, 'block'), may hold values from -0.5 to 2.7
- upper: float32 [2, 1024, 256], P(None, 'block'), may hold values from -0.5 to 2.7
- rhs: float32 [2, 8, 1024, 128], P(None, 'energy', 'block'), may hold values from -16 to 16
Outputs:
- solution: float32 [2, 8, 1024, 128], P(None, 'energy', 'block')
The draws below stay inside these ranges and needn't reach their ends.
All inputs are finite; a program needn't handle non-finite values.
Results may differ from the reference program's by a relative error of at most 0.0003.
Values sent between devices are 32-bit elements; how exact they have to be, the bound alone decides.
A program may use at most 64 MiB of HBM per device.

```python
import math
import jax
import jax.numpy as jnp
from jax import lax

BO = 256
NR = 128
NS_STEPS = 2
NE = 8
NB = 4
LEVELS = 2


def draw_onsite(key, part):
    first_key, second_key, third_key, fourth_key = jax.random.split(jax.random.fold_in(key, 11), 4)
    full_shape = (NE, NB * BO, BO)
    row_position = jnp.arange(NB * BO)[:, None] % BO
    column_position = jnp.arange(BO)[None, :]
    on_diagonal = (row_position == column_position).astype(jnp.float32)
    real_noise = jnp.clip(jax.random.normal(first_key, full_shape, jnp.float32), -4.0, 4.0)
    imag_noise = jnp.clip(jax.random.normal(second_key, full_shape, jnp.float32), -4.0, 4.0)
    real_diagonal = jax.random.uniform(third_key, full_shape, jnp.float32, 5.5, 6.5)
    imag_diagonal = jax.random.uniform(fourth_key, full_shape, jnp.float32, 0.2, 1.0)
    real_part = on_diagonal * real_diagonal + (1.0 - on_diagonal) * real_noise * (0.7 / math.sqrt(BO))
    imag_part = on_diagonal * imag_diagonal + (1.0 - on_diagonal) * imag_noise * (0.2 / math.sqrt(BO))
    return jnp.stack([real_part, imag_part])


def coupling_draw(key, draw_label):
    strength_key, real_key, imag_key = jax.random.split(jax.random.fold_in(key, draw_label), 3)
    full_shape = (NB * BO, BO)
    row_position = jnp.arange(NB * BO)[:, None] % BO
    column_position = jnp.arange(BO)[None, :]
    on_diagonal = (row_position == column_position).astype(jnp.float32)
    strength = jax.random.uniform(strength_key, full_shape, jnp.float32, 2.45, 2.7)
    real_noise = jnp.clip(jax.random.normal(real_key, full_shape, jnp.float32), -4.0, 4.0) * (0.7 / math.sqrt(BO))
    imag_noise = jnp.clip(jax.random.normal(imag_key, full_shape, jnp.float32), -4.0, 4.0) * (0.3 / math.sqrt(BO))
    real_part = on_diagonal * strength + (1.0 - on_diagonal) * real_noise
    return jnp.stack([real_part, imag_noise])


def draw_lower(key, part):
    return coupling_draw(key, 23)


def draw_upper(key, part):
    return coupling_draw(key, 37)


def block_scale(stream_key, dims, cuts, least, top_value):
    loudness, own = 1.0, jax.random.fold_in(stream_key, 6)
    for dim, shards_of in cuts:
        steps = jnp.exp(jax.random.uniform(jax.random.fold_in(own, dim), (shards_of,), jnp.float32, least / len(cuts), top_value / len(cuts)))
        loudness = loudness * jnp.repeat(steps, dims[dim] // shards_of).reshape([-1 if axis == dim else 1 for axis in range(len(dims))])
    return loudness


def bell_draw(rng, extent, deviation, reach, cuts=(), held_as=jnp.bfloat16):
    level = block_scale(rng, extent, cuts, -0.22, 0.18) if cuts else 1.0
    values = jax.random.normal(rng, extent, jnp.float32) * deviation * level
    return jnp.minimum(jnp.maximum(values, -reach), reach).astype(held_as)


def setup_inputs(seed: int = 0) -> dict:
    seeds = jax.random.split(jax.random.key(seed), 7)
    return {
        "g_lesser": bell_draw(seeds[0], (2, NE, NB * BO, BO), 0.12, 0.75, ((1, 8), (2, 4)), jnp.float32),
        "g_greater": bell_draw(seeds[1], (2, NE, NB * BO, BO), 0.12, 0.75, ((1, 8), (2, 4)), jnp.float32),
        "onsite": draw_onsite(jax.random.fold_in(seeds[6], 71), 0),
        "lower": draw_lower(jax.random.fold_in(seeds[6], 71), 0),
        "upper": draw_upper(jax.random.fold_in(seeds[6], 71), 0),
        "rhs": bell_draw(seeds[5], (2, NE, NB * BO, NR), 3.0, 16.0, ((1, 8), (2, 4)), jnp.float32),
    }


diagonal_guess = 5.0

def complex_product(left_factor, right_factor):
    exact_mode = lax.Precision.HIGHEST
    real_part = jnp.matmul(left_factor[0], right_factor[0], precision=exact_mode) - jnp.matmul(left_factor[1], right_factor[1], precision=exact_mode)
    imag_part = jnp.matmul(left_factor[0], right_factor[1], precision=exact_mode) + jnp.matmul(left_factor[1], right_factor[0], precision=exact_mode)
    return jnp.stack([real_part, imag_part])

def newton_inverse(matrix):
    block_order = matrix.shape[-1]
    identity = jnp.eye(block_order, dtype=jnp.float32)
    guess_real = jnp.broadcast_to(identity / diagonal_guess, matrix.shape[1:]).astype(jnp.float32)
    current = jnp.stack([guess_real, jnp.zeros_like(guess_real)])
    for sweep_index in range(NS_STEPS):
        product = complex_product(matrix, current)
        residue = jnp.stack([2.0 * identity - product[0], -product[1]])
        current = complex_product(current, residue)
    return current

def convolve(pair_arrays):
    lesser_part, greater_part = pair_arrays
    energies = lesser_part.shape[1]
    padded = jnp.concatenate([jnp.zeros_like(greater_part), greater_part], axis=1)

    def one_shift(offset):
        shifted = lax.dynamic_slice_in_dim(padded, (energies - offset).astype(jnp.int32), energies, 1)
        real_part = lax.optimization_barrier(jnp.sum(lesser_part[0] * shifted[0] - lesser_part[1] * shifted[1], axis=0))
        imag_part = lax.optimization_barrier(jnp.sum(lesser_part[0] * shifted[1] + lesser_part[1] * shifted[0], axis=0))
        return jnp.stack([real_part, imag_part])
    stacked = lax.map(one_shift, jnp.arange(energies, dtype=jnp.int32))
    return jnp.swapaxes(stacked, 0, 1) * (1.0 / math.sqrt(energies))

def from_before(values, stride):
    return jnp.concatenate([jnp.zeros_like(values[:, :, :stride]), values[:, :, :-stride]], axis=2)

def from_after(values, stride):
    return jnp.concatenate([values[:, :, stride:], jnp.zeros_like(values[:, :, :stride])], axis=2)

def reference(g_lesser, g_greater, onsite, lower, upper, rhs):
    lesser_blocks = g_lesser.reshape(2, NE, NB, BO, BO).transpose(2, 0, 1, 3, 4)
    greater_blocks = g_greater.reshape(2, NE, NB, BO, BO).transpose(2, 0, 1, 3, 4)
    polar = lax.map(convolve, (lesser_blocks, greater_blocks)).transpose(1, 2, 0, 3, 4)
    diag = onsite.reshape(2, NE, NB, BO, BO) - polar
    first_mask = (jnp.arange(NB) > 0).astype(jnp.float32)[None, :, None, None]
    last_mask = (jnp.arange(NB) < NB - 1).astype(jnp.float32)[None, :, None, None]
    lower_full = jnp.broadcast_to((lower.reshape(2, NB, BO, BO) * first_mask)[:, None], (2, NE, NB, BO, BO))
    upper_full = jnp.broadcast_to((upper.reshape(2, NB, BO, BO) * last_mask)[:, None], (2, NE, NB, BO, BO))
    source = rhs.reshape(2, NE, NB, BO, NR)
    for depth_index in range(LEVELS):
        stride = 1 << depth_index
        inverse = newton_inverse(diag)
        alpha = complex_product(inverse, lower_full)
        beta = complex_product(inverse, upper_full)
        rho = complex_product(inverse, source)
        alpha_left = from_before(alpha, stride)
        beta_left = from_before(beta, stride)
        rho_left = from_before(rho, stride)
        alpha_right = from_after(alpha, stride)
        beta_right = from_after(beta, stride)
        rho_right = from_after(rho, stride)
        diag = diag - complex_product(lower_full, beta_left) - complex_product(upper_full, alpha_right)
        source = source - complex_product(lower_full, rho_left) - complex_product(upper_full, rho_right)
        new_lower = -complex_product(lower_full, alpha_left)
        new_upper = -complex_product(upper_full, beta_right)
        lower_full = new_lower
        upper_full = new_upper
    solution = complex_product(newton_inverse(diag), source)
    return solution.reshape(2, NE, NB * BO, NR)
```

```python
import math

import jax
import jax.numpy as jnp
from jax import lax
from jax.sharding import PartitionSpec as P

diagonal_guess = 5.0
MODE = lax.Precision.HIGH


def real_product(a, b):
    return jnp.matmul(a, b, precision=MODE)


def product(a, b):
    ar, ai = a
    br, bi = b
    return (
        real_product(ar, br) - real_product(ai, bi),
        real_product(ar, bi) + real_product(ai, br),
    )


def parts(a):
    return a[0], a[1]


def plus(a, b):
    return a[0] + b[0], a[1] + b[1]


def minus(a, b):
    return a[0] - b[0], a[1] - b[1]


def wide(*pieces):
    return tuple(jnp.concatenate([p[k] for p in pieces], axis=-1) for k in (0, 1))


def cut(a, start, stop):
    return a[0][:, start:stop], a[1][:, start:stop]


def remainder(matrix):
    eye = jnp.eye(matrix[0].shape[-1], dtype=jnp.float32)
    return eye - matrix[0] * (1.0 / diagonal_guess), -matrix[1] * (1.0 / diagonal_guess)


def inverse(matrix):
    eye = jnp.eye(matrix[0].shape[-1], dtype=jnp.float32)
    b = remainder(matrix)
    square = product(b, b)
    cube = product(b, square)
    scale = 1.0 / diagonal_guess
    return (eye + b[0] + square[0] + cube[0]) * scale, (b[1] + square[1] + cube[1]) * scale


def solve(matrix, source):
    b = remainder(matrix)
    value = source
    for _ in range(3):
        value = plus(source, product(b, value))
    scale = 1.0 / diagonal_guess
    return value[0] * scale, value[1] * scale


def convolve(lesser, greater):
    energies = lesser.shape[1]
    scale = 1.0 / math.sqrt(energies)
    out = []
    for w in range(energies):
        count = energies - w
        a, b = lesser[:, w:], greater[:, :count]
        out.append(
            jnp.stack(
                [
                    jnp.sum(a[0] * b[0] - a[1] * b[1], axis=0),
                    jnp.sum(a[0] * b[1] + a[1] * b[0], axis=0),
                ]
            )
            * scale
        )
    return jnp.stack(out, axis=1)


def shifted(value, steps):
    count = lax.axis_size("block")
    leading, last = max(0, -steps), min(count, count - steps)
    pairs = [(k, k + steps) for k in range(leading, last)]
    return lax.ppermute(value, "block", pairs)


def shards(g_lesser, g_greater, onsite, lower, upper, rhs):
    index = lax.axis_index("block")
    count = lax.axis_size("block")
    levels = count.bit_length() - 1
    n = onsite.shape[-1]
    both = jnp.concatenate(
        [jnp.where(index > 0, lower, 0.0), jnp.where(index < count - 1, upper, 0.0)], axis=-1
    )
    early_left, early_right = shifted(both, 1), shifted(both, -1)
    rhs_left, rhs_right = shifted(rhs, 1), shifted(rhs, -1)

    lesser = lax.all_to_all(g_lesser, "energy", split_axis=2, concat_axis=1, tiled=True)
    greater = lax.all_to_all(g_greater, "energy", split_axis=2, concat_axis=1, tiled=True)
    polar = lax.all_to_all(
        convolve(lesser, greater), "energy", split_axis=1, concat_axis=2, tiled=True
    )
    diag = parts((onsite - polar)[:, 0])
    low, up = cut(parts(both), 0, n), cut(parts(both), n, 2 * n)
    source = parts(rhs[:, 0])
    for depth in range(levels):
        stride = 1 << depth
        inv = inverse(diag)
        if depth == levels - 1:
            coupling = tuple(jnp.where(index < stride, up[k], low[k]) for k in (0, 1))
            sent = product(inv, wide(coupling, source))
            swap = [(k, k ^ stride) for k in range(count)]
            got = parts(lax.ppermute(jnp.stack(sent), "block", swap))
            change = product(coupling, got)
            diag = minus(diag, cut(change, 0, n))
            source = minus(source, cut(change, n, None))
        elif depth == 0:
            packed = jnp.stack(inv)
            inv_left, inv_right = parts(shifted(packed, 1)), parts(shifted(packed, -1))
            before, after = parts(early_left), parts(early_right)
            t = product(low, inv_left)
            change = product(t, wide(before, parts(rhs_left[:, 0])))
            w = product(up, inv_right)
            other = product(w, wide(after, parts(rhs_right[:, 0])))
            diag = minus(minus(diag, cut(change, n, 2 * n)), cut(other, 0, n))
            source = minus(minus(source, cut(change, 2 * n, None)), cut(other, 2 * n, None))
            low = tuple(-v for v in cut(change, 0, n))
            up = tuple(-v for v in cut(other, n, 2 * n))
        else:
            sent = jnp.stack(product(inv, wide(low, up, source)))
            left, right = parts(shifted(sent, stride)), parts(shifted(sent, -stride))
            change, other = product(low, left), product(up, right)
            diag = minus(minus(diag, cut(change, n, 2 * n)), cut(other, 0, n))
            source = minus(minus(source, cut(change, 2 * n, None)), cut(other, 2 * n, None))
            low = tuple(-v for v in cut(change, 0, n))
            up = tuple(-v for v in cut(other, n, 2 * n))
    return jnp.stack(solve(diag, source))[:, None]


def solution(mesh):
    placed = (
        P(None, "energy", "block", None),
        P(None, "energy", "block", None),
        P(None, "energy", "block", None),
        P(None, "block", None),
        P(None, "block", None),
        P(None, "energy", "block", None),
    )
    return jax.shard_map(
        shards,
        mesh=mesh,
        in_specs=placed,
        out_specs=P(None, "energy", "block", None),
        check_vma=False,
    )
```

```python
import math

import jax
import jax.numpy as jnp
from jax import lax
from jax.experimental import pallas as pl
from jax.experimental.pallas import tpu as pltpu
from jax.sharding import PartitionSpec as P

diagonal_guess = 5.0
MODE = lax.Precision.HIGH
MESH = pl.DeviceIdType.MESH


def real_product(a, b):
    return jnp.matmul(a, b, precision=MODE)


def product(a, b):
    ar, ai = a
    br, bi = b
    return (
        real_product(ar, br) - real_product(ai, bi),
        real_product(ar, bi) + real_product(ai, br),
    )


def parts(a):
    return a[0], a[1]


def plus(a, b):
    return a[0] + b[0], a[1] + b[1]


def minus(a, b):
    return a[0] - b[0], a[1] - b[1]


def wide(*pieces):
    return tuple(jnp.concatenate([p[k] for p in pieces], axis=-1) for k in (0, 1))


def cut(a, start, stop):
    return a[0][:, start:stop], a[1][:, start:stop]


def remainder(matrix):
    eye = jnp.eye(matrix[0].shape[-1], dtype=jnp.float32)
    return eye - matrix[0] * (1.0 / diagonal_guess), -matrix[1] * (1.0 / diagonal_guess)


def inverse(matrix):
    eye = jnp.eye(matrix[0].shape[-1], dtype=jnp.float32)
    b = remainder(matrix)
    square = product(b, b)
    cube = product(b, square)
    scale = 1.0 / diagonal_guess
    return (eye + b[0] + square[0] + cube[0]) * scale, (b[1] + square[1] + cube[1]) * scale


def solve(matrix, source):
    b = remainder(matrix)
    value = source
    for _ in range(3):
        value = plus(source, product(b, value))
    scale = 1.0 / diagonal_guess
    return value[0] * scale, value[1] * scale


def front_kernel(
    gl, gg, onsite, lower, upper, rhs, diag, near_lu, near_s,
    lu, gl_all, gg_all, res, pol,
    in_send, in_recv, out_send, out_recv, lu_send, lu_recv, hop_send, hop_recv,
    mate_send, mate_recv, local,
):
    e, i = lax.axis_index("energy"), lax.axis_index("block")
    energies, count = lax.axis_size("energy"), lax.axis_size("block")
    share = gl.shape[2] // energies
    c, p = lax.rem(e, 2), lax.rem(i, 2)
    mate, side = e + 1 - 2 * c, 1 - p
    pair, onward, behind = i + 1 - 2 * p, i + 2 - 4 * p, i - 2 + 4 * p
    has_onward = jnp.logical_and(onward >= 0, onward < count)
    has_behind = jnp.logical_and(behind >= 0, behind < count)

    fill = [pltpu.make_async_copy((lower, upper)[k], lu.at[k], local.at[k]) for k in (0, 1)]
    for copy in fill:
        copy.start()
    barrier = pltpu.get_barrier_semaphore()
    for k in range(1, energies):
        pl.semaphore_signal(barrier, inc=1, device_id={"energy": lax.rem(e + k, energies)}, device_id_type=MESH)
    pl.semaphore_signal(barrier, inc=1, device_id={"block": pair}, device_id_type=MESH)

    @pl.when(has_onward)
    def _():
        pl.semaphore_signal(barrier, inc=1, device_id={"block": onward}, device_id_type=MESH)

    @pl.when(has_behind)
    def _():
        pl.semaphore_signal(barrier, inc=1, device_id={"block": behind}, device_id_type=MESH)

    pl.semaphore_wait(barrier, energies + has_onward.astype(jnp.int32) + has_behind.astype(jnp.int32))

    def remote(src, dst, send, recv, **where):
        return pltpu.make_async_remote_copy(
            src_ref=src, dst_ref=dst, send_sem=send, recv_sem=recv, device_id=where, device_id_type=MESH
        )

    def in_copy(k, q, source):
        src, dst = ((gl, gl_all), (gg, gg_all))[k]
        rows = src.at[:, 0, pl.ds(q * share, share), :]
        return remote(rows, dst.at[source], in_send.at[k, q], in_recv.at[k, source], energy=q)

    def out_copy(w, source):
        return remote(res.at[w], pol.at[source], out_send.at[w], out_recv.at[source], energy=w)

    for copy in fill:
        copy.wait()
    for k in (0, 1):
        for q in range(energies):

            @pl.when(q != e)
            def _():
                in_copy(k, q, e).start()

    own = []
    for k, (src, dst) in enumerate(((gl, gl_all), (gg, gg_all))):
        rows = src.at[:, 0, pl.ds(pl.multiple_of(e * share, 8), share), :]
        own.append(pltpu.make_async_copy(rows, dst.at[e], local.at[k]))
        own[-1].start()

    mine = (lu.at[c, 0], lu.at[c, 1], rhs.at[:, 0])

    def slot(s, k):
        return near_s.at[s] if k == 2 else near_lu.at[s, c, k]

    direct = [remote(mine[k], slot(p, k), lu_send.at[k], lu_recv.at[k], block=pair) for k in range(3)]
    hops = [remote(slot(side, k), slot(p, k), hop_send.at[k], hop_recv.at[k], block=onward) for k in range(3)]
    for copy in direct:
        copy.start()
    shared = [
        remote(slot(s, k), slot(s, k), mate_send.at[j, k], mate_recv.at[j, k], energy=mate)
        for j, s in enumerate((side, p))
        for k in (0, 1)
    ]
    for k in range(3):
        direct[k].wait_recv()

        @pl.when(has_onward)
        def _():
            hops[k].start()

        if k < 2:
            shared[k].start()

    for copy in own:
        copy.wait()
    for k in (0, 1):
        for q in range(energies):

            @pl.when(q != e)
            def _():
                in_copy(k, q, q).wait_recv()

    scale = 1.0 / math.sqrt(energies)
    for w in list(range(energies)):

        def step(row, carry, w=w):
            rows = pl.ds(pl.multiple_of(row * 8, 8), 8)
            real = imag = None
            for k in range(w, energies):
                a, b = gl_all[k, 0, rows], gl_all[k, 1, rows]
                x, y = gg_all[k - w, 0, rows], gg_all[k - w, 1, rows]
                s, t = a * x - b * y, a * y + b * x
                real, imag = (s, t) if real is None else (real + s, imag + t)
            res[w, 0, rows] = real * scale
            res[w, 1, rows] = imag * scale
            return carry

        lax.fori_loop(0, share // 8, step, 0)

        @pl.when(w != e)
        def _():
            out_copy(w, e).start()

    keep = pltpu.make_async_copy(res.at[e], pol.at[e], local.at[0])
    keep.start()

    @pl.when(has_behind)
    def _():
        for k in range(3):
            hops[k].wait_recv()
            if k < 2:
                shared[2 + k].start()

    keep.wait()
    for q in range(energies):

        @pl.when(q != e)
        def _():
            out_copy(q, q).wait_recv()

        rows = pl.ds(q * share, share)
        for k in (0, 1):
            diag[k, rows] = onsite[k, 0, rows] - pol[q, k]

    for k in range(2):
        shared[k].wait_recv()

    @pl.when(has_behind)
    def _():
        for k in range(2):
            shared[2 + k].wait()

    for k in range(2):
        shared[k].wait_send()
    for k in range(3):
        direct[k].wait_send()

        @pl.when(has_onward)
        def _():
            hops[k].wait_send()

    for q in range(energies):

        @pl.when(q != e)
        def _():
            in_copy(0, q, e).wait_send()
            in_copy(1, q, e).wait_send()
            out_copy(q, e).wait_send()


def front(g_lesser, g_greater, onsite, lower, upper, rhs):
    energies = lax.axis_size("energy")
    n, columns = onsite.shape[2], rhs.shape[-1]
    share = n // energies
    vmem = pl.BlockSpec(memory_space=pltpu.VMEM)
    f32 = jnp.float32
    dma = pltpu.SemaphoreType.DMA
    pieces = pltpu.VMEM((energies, 2, share, n), f32)
    return pl.pallas_call(
        front_kernel,
        name="front",
        out_shape=(
            jax.ShapeDtypeStruct((2, n, n), f32),
            jax.ShapeDtypeStruct((2, 2, 2, n, n), f32),
            jax.ShapeDtypeStruct((2, 2, n, columns), f32),
        ),
        in_specs=[vmem] * 6,
        out_specs=(vmem,) * 3,
        scratch_shapes=[
            pltpu.VMEM((2, 2, n, n), f32),
            pieces, pieces, pieces, pieces,
            dma((2, energies)), dma((2, energies)), dma((energies,)), dma((energies,)),
            dma((3,)), dma((3,)), dma((3,)), dma((3,)),
            dma((2, 2)), dma((2, 2)), dma((2,)),
        ],
        compiler_params=pltpu.CompilerParams(collective_id=0, has_side_effects=True),
    )(g_lesser, g_greater, onsite, lower, upper, rhs)


def shifted(value, steps):
    count = lax.axis_size("block")
    leading, last = max(0, -steps), min(count, count - steps)
    pairs = [(k, k + steps) for k in range(leading, last)]
    return lax.ppermute(value, "block", pairs)


def shards(g_lesser, g_greater, onsite, lower, upper, rhs):
    index = lax.axis_index("block")
    count = lax.axis_size("block")
    levels = count.bit_length() - 1
    n = onsite.shape[-1]
    both = jnp.concatenate(
        [jnp.where(index > 0, lower, 0.0), jnp.where(index < count - 1, upper, 0.0)], axis=-1
    )
    diag, near_lu, near_s = front(g_lesser, g_greater, onsite, lower, upper, rhs)
    diag = parts(diag)
    first, final = index < 2, index >= count - 2
    low, up = cut(parts(both), 0, n), cut(parts(both), n, 2 * n)
    source = parts(rhs[:, 0])
    for depth in range(levels):
        stride = 1 << depth
        inv = inverse(diag)
        if depth == levels - 1:
            coupling = tuple(jnp.where(index < stride, up[k], low[k]) for k in (0, 1))
            sent = product(inv, wide(coupling, source))
            swap = [(k, k ^ stride) for k in range(count)]
            got = parts(lax.ppermute(jnp.stack(sent), "block", swap))
            change = product(coupling, got)
            diag = minus(diag, cut(change, 0, n))
            source = minus(source, cut(change, n, None))
        elif depth == 0:
            packed = jnp.stack(inv)
            inv_left, inv_right = parts(shifted(packed, 1)), parts(shifted(packed, -1))
            t, w = product(low, inv_left), product(up, inv_right)
            lu_l, lu_r = near_lu[0], near_lu[1]
            change = product(t, wide(parts(lu_l[0]), parts(lu_l[1]), parts(near_s[0])))
            other = product(w, wide(parts(lu_r[0]), parts(lu_r[1]), parts(near_s[1])))
            change = tuple(jnp.where(index > 0, v, 0.0) for v in change)
            other = tuple(jnp.where(index < count - 1, v, 0.0) for v in other)
            diag = minus(minus(diag, cut(change, n, 2 * n)), cut(other, 0, n))
            source = minus(minus(source, cut(change, 2 * n, None)), cut(other, 2 * n, None))
            low = tuple(jnp.where(first, 0.0, -v) for v in cut(change, 0, n))
            up = tuple(jnp.where(final, 0.0, -v) for v in cut(other, n, 2 * n))
        else:
            sent = jnp.stack(product(inv, wide(low, up, source)))
            left, right = parts(shifted(sent, stride)), parts(shifted(sent, -stride))
            change, other = product(low, left), product(up, right)
            diag = minus(minus(diag, cut(change, n, 2 * n)), cut(other, 0, n))
            source = minus(minus(source, cut(change, 2 * n, None)), cut(other, 2 * n, None))
            low = tuple(-v for v in cut(change, 0, n))
            up = tuple(-v for v in cut(other, n, 2 * n))
    return jnp.stack(solve(diag, source))[:, None]


def solution(mesh):
    placed = (
        P(None, "energy", "block", None),
        P(None, "energy", "block", None),
        P(None, "energy", "block", None),
        P(None, "block", None),
        P(None, "block", None),
        P(None, "energy", "block", None),
    )
    return jax.shard_map(
        shards,
        mesh=mesh,
        in_specs=placed,
        out_specs=P(None, "energy", "block", None),
        check_vma=False,
    )
```

```python
import math

import jax
import jax.numpy as jnp
from jax import lax
from jax.experimental import pallas as pl
from jax.experimental.pallas import tpu as pltpu
from jax.sharding import PartitionSpec as P

diagonal_guess = 5.0
MODE = lax.Precision.HIGH
MESH = pl.DeviceIdType.MESH


def real_product(a, b):
    return jnp.matmul(a, b, precision=MODE)


def product(a, b):
    ar, ai = a
    br, bi = b
    return (
        real_product(ar, br) - real_product(ai, bi),
        real_product(ar, bi) + real_product(ai, br),
    )


def parts(a):
    return a[0], a[1]


def plus(a, b):
    return a[0] + b[0], a[1] + b[1]


def minus(a, b):
    return a[0] - b[0], a[1] - b[1]


def wide(*pieces):
    return tuple(jnp.concatenate([p[k] for p in pieces], axis=-1) for k in (0, 1))


def cut(a, start, stop):
    return a[0][:, start:stop], a[1][:, start:stop]


def remainder(matrix):
    eye = jnp.eye(matrix[0].shape[-1], dtype=jnp.float32)
    return eye - matrix[0] * (1.0 / diagonal_guess), -matrix[1] * (1.0 / diagonal_guess)


def inverse(matrix):
    eye = jnp.eye(matrix[0].shape[-1], dtype=jnp.float32)
    b = remainder(matrix)
    square = product(b, b)
    cube = product(b, square)
    scale = 1.0 / diagonal_guess
    return (eye + b[0] + square[0] + cube[0]) * scale, (b[1] + square[1] + cube[1]) * scale


def solve(matrix, source):
    b = remainder(matrix)
    value = source
    for _ in range(3):
        value = plus(source, product(b, value))
    scale = 1.0 / diagonal_guess
    return value[0] * scale, value[1] * scale


def front_kernel(
    gl, gg, onsite, lower, upper, rhs, diag, near_lu, near_s,
    lu, gl_all, gg_all, res, pol,
    in_send, in_recv, out_send, out_recv, lu_send, lu_recv, hop_send, hop_recv,
    mate_send, mate_recv, local,
):
    e, i = lax.axis_index("energy"), lax.axis_index("block")
    energies, count = lax.axis_size("energy"), lax.axis_size("block")
    share = gl.shape[2] // energies
    c, p = lax.rem(e, 2), lax.rem(i, 2)
    mate, side = e + 1 - 2 * c, 1 - p
    pair, onward, behind = i + 1 - 2 * p, i + 2 - 4 * p, i - 2 + 4 * p
    has_onward = jnp.logical_and(onward >= 0, onward < count)
    has_behind = jnp.logical_and(behind >= 0, behind < count)

    fill = [pltpu.make_async_copy((lower, upper)[k], lu.at[k], local.at[k]) for k in (0, 1)]
    for copy in fill:
        copy.start()
    barrier = pltpu.get_barrier_semaphore()
    for k in range(1, energies):
        pl.semaphore_signal(barrier, inc=1, device_id={"energy": lax.rem(e + k, energies)}, device_id_type=MESH)
    pl.semaphore_signal(barrier, inc=1, device_id={"block": pair}, device_id_type=MESH)

    @pl.when(has_onward)
    def _():
        pl.semaphore_signal(barrier, inc=1, device_id={"block": onward}, device_id_type=MESH)

    @pl.when(has_behind)
    def _():
        pl.semaphore_signal(barrier, inc=1, device_id={"block": behind}, device_id_type=MESH)

    pl.semaphore_wait(barrier, energies + has_onward.astype(jnp.int32) + has_behind.astype(jnp.int32))

    def remote(src, dst, send, recv, **where):
        return pltpu.make_async_remote_copy(
            src_ref=src, dst_ref=dst, send_sem=send, recv_sem=recv, device_id=where, device_id_type=MESH
        )

    def in_copy(k, q, source):
        src, dst = ((gl, gl_all), (gg, gg_all))[k]
        rows = src.at[:, 0, pl.ds(q * share, share), :]
        return remote(rows, dst.at[source], in_send.at[k, q], in_recv.at[k, source], energy=q)

    def out_copy(w, source):
        return remote(res.at[w], pol.at[source], out_send.at[w], out_recv.at[source], energy=w)

    for copy in fill:
        copy.wait()
    for k in (0, 1):
        for q in range(energies):

            @pl.when(q != e)
            def _():
                in_copy(k, q, e).start()

    own = []
    for k, (src, dst) in enumerate(((gl, gl_all), (gg, gg_all))):
        rows = src.at[:, 0, pl.ds(pl.multiple_of(e * share, 8), share), :]
        own.append(pltpu.make_async_copy(rows, dst.at[e], local.at[k]))
        own[-1].start()

    mine = (lu.at[c, 0], lu.at[c, 1], rhs.at[:, 0])

    def slot(s, k):
        return near_s.at[s] if k == 2 else near_lu.at[s, c, k]

    direct = [remote(mine[k], slot(p, k), lu_send.at[k], lu_recv.at[k], block=pair) for k in range(3)]
    hops = [remote(slot(side, k), slot(p, k), hop_send.at[k], hop_recv.at[k], block=onward) for k in range(3)]
    for copy in direct:
        copy.start()
    shared = [
        remote(slot(s, k), slot(s, k), mate_send.at[j, k], mate_recv.at[j, k], energy=mate)
        for j, s in enumerate((side, p))
        for k in (0, 1)
    ]
    for k in range(3):
        direct[k].wait_recv()

        @pl.when(has_onward)
        def _():
            hops[k].start()

        if k < 2:
            shared[k].start()

    for copy in own:
        copy.wait()
    for k in (0, 1):
        for q in range(energies):

            @pl.when(q != e)
            def _():
                in_copy(k, q, q).wait_recv()

    scale = 1.0 / math.sqrt(energies)
    for w in list(range(energies)):

        def step(row, carry, w=w):
            rows = pl.ds(pl.multiple_of(row * 8, 8), 8)
            real = imag = None
            for k in range(w, energies):
                a, b = gl_all[k, 0, rows], gl_all[k, 1, rows]
                x, y = gg_all[k - w, 0, rows], gg_all[k - w, 1, rows]
                s, t = a * x - b * y, a * y + b * x
                real, imag = (s, t) if real is None else (real + s, imag + t)
            res[w, 0, rows] = real * scale
            res[w, 1, rows] = imag * scale
            return carry

        lax.fori_loop(0, share // 8, step, 0)

        @pl.when(w != e)
        def _():
            out_copy(w, e).start()

    keep = pltpu.make_async_copy(res.at[e], pol.at[e], local.at[0])
    keep.start()

    @pl.when(has_behind)
    def _():
        for k in range(3):
            hops[k].wait_recv()
            if k < 2:
                shared[2 + k].start()

    keep.wait()
    for q in range(energies):

        @pl.when(q != e)
        def _():
            out_copy(q, q).wait_recv()

        rows = pl.ds(q * share, share)
        for k in (0, 1):
            diag[k, rows] = onsite[k, 0, rows] - pol[q, k]

    for k in range(2):
        shared[k].wait_recv()

    @pl.when(has_behind)
    def _():
        for k in range(2):
            shared[2 + k].wait()

    for k in range(2):
        shared[k].wait_send()
    for k in range(3):
        direct[k].wait_send()

        @pl.when(has_onward)
        def _():
            hops[k].wait_send()

    for q in range(energies):

        @pl.when(q != e)
        def _():
            in_copy(0, q, e).wait_send()
            in_copy(1, q, e).wait_send()
            out_copy(q, e).wait_send()


def front(g_lesser, g_greater, onsite, lower, upper, rhs):
    energies = lax.axis_size("energy")
    n, columns = onsite.shape[2], rhs.shape[-1]
    share = n // energies
    vmem = pl.BlockSpec(memory_space=pltpu.VMEM)
    f32 = jnp.float32
    dma = pltpu.SemaphoreType.DMA
    pieces = pltpu.VMEM((energies, 2, share, n), f32)
    return pl.pallas_call(
        front_kernel,
        name="front",
        out_shape=(
            jax.ShapeDtypeStruct((2, n, n), f32),
            jax.ShapeDtypeStruct((2, 2, 2, n, n), f32),
            jax.ShapeDtypeStruct((2, 2, n, columns), f32),
        ),
        in_specs=[vmem] * 6,
        out_specs=(vmem,) * 3,
        scratch_shapes=[
            pltpu.VMEM((2, 2, n, n), f32),
            pieces, pieces, pieces, pieces,
            dma((2, energies)), dma((2, energies)), dma((energies,)), dma((energies,)),
            dma((3,)), dma((3,)), dma((3,)), dma((3,)),
            dma((2, 2)), dma((2, 2)), dma((2,)),
        ],
        compiler_params=pltpu.CompilerParams(collective_id=0, has_side_effects=True),
    )(g_lesser, g_greater, onsite, lower, upper, rhs)


def halves(x):
    high = x.astype(jnp.bfloat16)
    return high, (x - high.astype(jnp.float32)).astype(jnp.bfloat16)


def factor(a):
    return halves(a[0]), halves(a[1]), halves(a[0] + a[1])


def three_pass(a, b):
    dot = lambda u, v: jnp.dot(u, v, preferred_element_type=jnp.float32)
    return dot(a[0], b[0]) + (dot(a[0], b[1]) + dot(a[1], b[0]))


def times(a, b):
    first, second, third = (three_pass(a[k], b[k]) for k in range(3))
    return first - second, third - first - second


def inverse_of(matrix):
    eye_rows = lax.broadcasted_iota(jnp.int32, matrix[0].shape, 0)
    eye_columns = lax.broadcasted_iota(jnp.int32, matrix[0].shape, 1)
    eye = jnp.where(eye_rows == eye_columns, 1.0, 0.0)
    scale = 1.0 / diagonal_guess
    b = eye - matrix[0] * scale, -matrix[1] * scale
    fb = factor(b)
    square = times(fb, fb)
    cube = times(fb, factor(square))
    return (eye + b[0] + square[0] + cube[0]) * scale, (b[1] + square[1] + cube[1]) * scale


def back_kernel(
    diag, lower, upper, near_lu, near_s, rhs, out, d, s, lu, x, near_x, g, got,
    direct_send, direct_recv, hop_send, hop_recv, g_send, g_recv,
):
    i, count = lax.axis_index("block"), lax.axis_size("block")
    n, columns = d.shape[-1], s.shape[-1]
    p, stride = lax.rem(i, 2), count // 2
    side = 1 - p
    pair, onward, behind = i + 1 - 2 * p, i + 2 - 4 * p, i - 2 + 4 * p
    has_onward = jnp.logical_and(onward >= 0, onward < count)
    has_behind = jnp.logical_and(behind >= 0, behind < count)
    partner = lax.rem(i + stride, count)

    barrier = pltpu.get_barrier_semaphore()
    for where in (pair, partner):
        pl.semaphore_signal(barrier, inc=1, device_id={"block": where}, device_id_type=MESH)
    for there, where in ((has_onward, onward), (has_behind, behind)):

        @pl.when(there)
        def _():
            pl.semaphore_signal(barrier, inc=1, device_id={"block": where}, device_id_type=MESH)

    pl.semaphore_wait(barrier, 2 + has_onward.astype(jnp.int32) + has_behind.astype(jnp.int32))

    def remote(src, dst, send, recv, where):
        return pltpu.make_async_remote_copy(
            src_ref=src, dst_ref=dst, send_sem=send, recv_sem=recv, device_id={"block": where}, device_id_type=MESH
        )

    value = inverse_of((diag[0], diag[1]))
    x[0], x[1] = value
    tile = n // 4
    direct, hops = [], []
    for k in range(4):
        rows = pl.ds(k * tile, tile)
        direct.append(remote(x.at[:, rows], near_x.at[p, :, rows], direct_send.at[k], direct_recv.at[k], pair))
        hops.append(remote(near_x.at[side, :, rows], near_x.at[p, :, rows], hop_send.at[k], hop_recv.at[k], onward))
        direct[k].start()
    d[...] = diag[...]
    s[...] = rhs[:, 0]
    for k in (0, 1):
        lu[0, k], lu[1, k] = lower[k], upper[k]
    for k in range(4):
        direct[k].wait_recv()

        @pl.when(has_onward)
        def _():
            hops[k].start()

    def update(which, kept):
        t = factor(times(factor((lu[which, 0], lu[which, 1])), factor((near_x[which, 0], near_x[which, 1]))))
        v = times(t, factor((near_lu[which, 1 - which, 0], near_lu[which, 1 - which, 1])))
        r = times(t, factor((near_s[which, 0], near_s[which, 1])))
        for k in (0, 1):
            d[k] = d[k] - v[k]
            s[k] = s[k] - r[k]

        @pl.when(kept)
        def _():
            c = times(t, factor((near_lu[which, which, 0], near_lu[which, which, 1])))
            for k in (0, 1):
                lu[which, k] = -c[k]

    update(side, has_onward)

    @pl.when(has_behind)
    def _():
        for k in range(4):
            hops[k].wait_recv()
        update(p, has_behind)

    live = jnp.where(i < stride, 1, 0)
    inv = factor(inverse_of((d[0], d[1])))
    chunks = n // columns
    swaps = [remote(g.at[k], got.at[k], g_send.at[k], g_recv.at[k], partner) for k in range(chunks + 1)]
    for k in range(chunks + 1):
        if k == chunks:
            right = s[0], s[1]
        else:
            right = tuple(lu[live, m, :, k * columns : (k + 1) * columns] for m in (0, 1))
        part = times(inv, factor(right))
        g[k, 0], g[k, 1] = part
        swaps[k].start()
    coupling = factor((lu[live, 0], lu[live, 1]))
    for k in range(chunks + 1):
        swaps[k].wait_recv()
        change = times(coupling, factor((got[k, 0], got[k, 1])))
        for m in (0, 1):
            if k == chunks:
                s[m] = s[m] - change[m]
            else:
                cols = slice(k * columns, (k + 1) * columns)
                d[m, :, cols] = d[m, :, cols] - change[m]

    rows = lax.broadcasted_iota(jnp.int32, (n, n), 0)
    eye = jnp.where(rows == lax.broadcasted_iota(jnp.int32, (n, n), 1), 1.0, 0.0)
    scale = 1.0 / diagonal_guess
    b = factor((eye - d[0] * scale, -d[1] * scale))
    source = s[0], s[1]
    value = source
    for _ in range(3):
        value = plus(source, times(b, factor(value)))
    out[0, 0], out[1, 0] = value[0] * scale, value[1] * scale
    for k in range(4):
        direct[k].wait_send()

        @pl.when(has_onward)
        def _():
            hops[k].wait_send()

    for k in range(chunks + 1):
        swaps[k].wait_send()


def back(diag, lower, upper, near_lu, near_s, rhs):
    n, columns = diag.shape[-1], rhs.shape[-1]
    vmem = pl.BlockSpec(memory_space=pltpu.VMEM)
    f32 = jnp.float32
    dma = pltpu.SemaphoreType.DMA
    chunks = n // columns + 1
    return pl.pallas_call(
        back_kernel,
        name="back",
        out_shape=jax.ShapeDtypeStruct((2, 1, n, columns), f32),
        in_specs=[vmem] * 6,
        out_specs=vmem,
        scratch_shapes=[
            pltpu.VMEM((2, n, n), f32),
            pltpu.VMEM((2, n, columns), f32),
            pltpu.VMEM((2, 2, n, n), f32),
            pltpu.VMEM((2, n, n), f32),
            pltpu.VMEM((2, 2, n, n), f32),
            pltpu.VMEM((chunks, 2, n, columns), f32),
            pltpu.VMEM((chunks, 2, n, columns), f32),
            dma((4,)), dma((4,)), dma((4,)), dma((4,)), dma((chunks,)), dma((chunks,)),
        ],
        compiler_params=pltpu.CompilerParams(collective_id=1, has_side_effects=True),
    )(diag, lower, upper, near_lu, near_s, rhs)


def shifted(value, steps):
    count = lax.axis_size("block")
    leading, last = max(0, -steps), min(count, count - steps)
    pairs = [(k, k + steps) for k in range(leading, last)]
    return lax.ppermute(value, "block", pairs)


def shards(g_lesser, g_greater, onsite, lower, upper, rhs):
    index = lax.axis_index("block")
    count = lax.axis_size("block")
    levels = count.bit_length() - 1
    n = onsite.shape[-1]
    both = jnp.concatenate(
        [jnp.where(index > 0, lower, 0.0), jnp.where(index < count - 1, upper, 0.0)], axis=-1
    )
    diag, near_lu, near_s = front(g_lesser, g_greater, onsite, lower, upper, rhs)
    if levels == 2:
        return back(diag, lower, upper, near_lu, near_s, rhs)
    diag = parts(diag)
    first, final = index < 2, index >= count - 2
    low, up = cut(parts(both), 0, n), cut(parts(both), n, 2 * n)
    source = parts(rhs[:, 0])
    for depth in range(levels):
        stride = 1 << depth
        inv = inverse(diag)
        if depth == levels - 1:
            coupling = tuple(jnp.where(index < stride, up[k], low[k]) for k in (0, 1))
            sent = product(inv, wide(coupling, source))
            swap = [(k, k ^ stride) for k in range(count)]
            got = parts(lax.ppermute(jnp.stack(sent), "block", swap))
            change = product(coupling, got)
            diag = minus(diag, cut(change, 0, n))
            source = minus(source, cut(change, n, None))
        elif depth == 0:
            packed = jnp.stack(inv)
            inv_left, inv_right = parts(shifted(packed, 1)), parts(shifted(packed, -1))
            t, w = product(low, inv_left), product(up, inv_right)
            lu_l, lu_r = near_lu[0], near_lu[1]
            change = product(t, wide(parts(lu_l[0]), parts(lu_l[1]), parts(near_s[0])))
            other = product(w, wide(parts(lu_r[0]), parts(lu_r[1]), parts(near_s[1])))
            change = tuple(jnp.where(index > 0, v, 0.0) for v in change)
            other = tuple(jnp.where(index < count - 1, v, 0.0) for v in other)
            diag = minus(minus(diag, cut(change, n, 2 * n)), cut(other, 0, n))
            source = minus(minus(source, cut(change, 2 * n, None)), cut(other, 2 * n, None))
            low = tuple(jnp.where(first, 0.0, -v) for v in cut(change, 0, n))
            up = tuple(jnp.where(final, 0.0, -v) for v in cut(other, n, 2 * n))
        else:
            sent = jnp.stack(product(inv, wide(low, up, source)))
            left, right = parts(shifted(sent, stride)), parts(shifted(sent, -stride))
            change, other = product(low, left), product(up, right)
            diag = minus(minus(diag, cut(change, n, 2 * n)), cut(other, 0, n))
            source = minus(minus(source, cut(change, 2 * n, None)), cut(other, 2 * n, None))
            low = tuple(-v for v in cut(change, 0, n))
            up = tuple(-v for v in cut(other, n, 2 * n))
    return jnp.stack(solve(diag, source))[:, None]


def solution(mesh):
    placed = (
        P(None, "energy", "block", None),
        P(None, "energy", "block", None),
        P(None, "energy", "block", None),
        P(None, "block", None),
        P(None, "block", None),
        P(None, "energy", "block", None),
    )
    return jax.shard_map(
        shards,
        mesh=mesh,
        in_specs=placed,
        out_specs=P(None, "energy", "block", None),
        check_vma=False,
    )
```

```python
import math

import jax
import jax.numpy as jnp
from jax import lax
from jax.experimental import pallas as pl
from jax.experimental.pallas import tpu as pltpu
from jax.sharding import PartitionSpec as P

diagonal_guess = 5.0
MODE = lax.Precision.HIGH
MESH = pl.DeviceIdType.MESH


def real_product(a, b):
    return jnp.matmul(a, b, precision=MODE)


def product(a, b):
    ar, ai = a
    br, bi = b
    return (
        real_product(ar, br) - real_product(ai, bi),
        real_product(ar, bi) + real_product(ai, br),
    )


def parts(a):
    return a[0], a[1]


def plus(a, b):
    return a[0] + b[0], a[1] + b[1]


def minus(a, b):
    return a[0] - b[0], a[1] - b[1]


def wide(*pieces):
    return tuple(jnp.concatenate([p[k] for p in pieces], axis=-1) for k in (0, 1))


def cut(a, start, stop):
    return a[0][:, start:stop], a[1][:, start:stop]


def remainder(matrix):
    eye = jnp.eye(matrix[0].shape[-1], dtype=jnp.float32)
    return eye - matrix[0] * (1.0 / diagonal_guess), -matrix[1] * (1.0 / diagonal_guess)


def inverse(matrix):
    eye = jnp.eye(matrix[0].shape[-1], dtype=jnp.float32)
    b = remainder(matrix)
    square = product(b, b)
    cube = product(b, square)
    scale = 1.0 / diagonal_guess
    return (eye + b[0] + square[0] + cube[0]) * scale, (b[1] + square[1] + cube[1]) * scale


def solve(matrix, source):
    b = remainder(matrix)
    value = source
    for _ in range(3):
        value = plus(source, product(b, value))
    scale = 1.0 / diagonal_guess
    return value[0] * scale, value[1] * scale


def front_kernel(
    gl, gg, onsite, lower, upper, rhs, diag, near_lu, near_s,
    lu, gl_all, gg_all, res, pol,
    in_send, in_recv, out_send, out_recv, lu_send, lu_recv, hop_send, hop_recv,
    mate_send, mate_recv, local, rows_out=None, partner=None,
):
    e, i = lax.axis_index("energy"), lax.axis_index("block")
    energies, count = lax.axis_size("energy"), lax.axis_size("block")
    share = gl.shape[2] // energies
    c, p = lax.rem(e, 2), lax.rem(i, 2)
    mate, side = e + 1 - 2 * c, 1 - p
    pair, onward, behind = i + 1 - 2 * p, i + 2 - 4 * p, i - 2 + 4 * p
    has_onward = jnp.logical_and(onward >= 0, onward < count)
    has_behind = jnp.logical_and(behind >= 0, behind < count)

    fill = [pltpu.make_async_copy((lower, upper)[k], lu.at[k], local.at[k]) for k in (0, 1)]
    for copy in fill:
        copy.start()
    barrier = pltpu.get_barrier_semaphore()
    for k in range(1, energies):
        pl.semaphore_signal(barrier, inc=1, device_id={"energy": lax.rem(e + k, energies)}, device_id_type=MESH)
    pl.semaphore_signal(barrier, inc=1, device_id={"block": pair}, device_id_type=MESH)

    @pl.when(has_onward)
    def _():
        pl.semaphore_signal(barrier, inc=1, device_id={"block": onward}, device_id_type=MESH)

    @pl.when(has_behind)
    def _():
        pl.semaphore_signal(barrier, inc=1, device_id={"block": behind}, device_id_type=MESH)

    peers = energies
    if partner is not None:
        peers = energies + 1
        pl.semaphore_signal(barrier, inc=1, device_id={"block": partner}, device_id_type=MESH)
    pl.semaphore_wait(barrier, peers + has_onward.astype(jnp.int32) + has_behind.astype(jnp.int32))

    def remote(src, dst, send, recv, **where):
        return pltpu.make_async_remote_copy(
            src_ref=src, dst_ref=dst, send_sem=send, recv_sem=recv, device_id=where, device_id_type=MESH
        )

    def in_copy(k, q, source):
        src, dst = ((gl, gl_all), (gg, gg_all))[k]
        rows = src.at[:, 0, pl.ds(q * share, share), :]
        return remote(rows, dst.at[source], in_send.at[k, q], in_recv.at[k, source], energy=q)

    def out_copy(w, source):
        return remote(res.at[w], pol.at[source], out_send.at[w], out_recv.at[source], energy=w)

    for copy in fill:
        copy.wait()
    for k in (0, 1):
        for q in range(energies):

            @pl.when(q != e)
            def _():
                in_copy(k, q, e).start()

    own = []
    for k, (src, dst) in enumerate(((gl, gl_all), (gg, gg_all))):
        rows = src.at[:, 0, pl.ds(pl.multiple_of(e * share, 8), share), :]
        own.append(pltpu.make_async_copy(rows, dst.at[e], local.at[k]))
        own[-1].start()

    mine = (lu.at[c, 0], lu.at[c, 1], rhs.at[:, 0])

    def slot(s, k):
        return near_s.at[s] if k == 2 else near_lu.at[s, c, k]

    direct = [remote(mine[k], slot(p, k), lu_send.at[k], lu_recv.at[k], block=pair) for k in range(3)]
    hops = [remote(slot(side, k), slot(p, k), hop_send.at[k], hop_recv.at[k], block=onward) for k in range(3)]
    for copy in direct:
        copy.start()
    shared = [
        remote(slot(s, k), slot(s, k), mate_send.at[j, k], mate_recv.at[j, k], energy=mate)
        for j, s in enumerate((side, p))
        for k in (0, 1)
    ]
    for k in range(3):
        direct[k].wait_recv()

        @pl.when(has_onward)
        def _():
            hops[k].start()

        if k < 2:
            shared[k].start()

    for copy in own:
        copy.wait()
    for k in (0, 1):
        for q in range(energies):

            @pl.when(q != e)
            def _():
                in_copy(k, q, q).wait_recv()

    scale = 1.0 / math.sqrt(energies)
    for w in list(range(energies)):

        def step(row, carry, w=w):
            rows = pl.ds(pl.multiple_of(row * 8, 8), 8)
            real = imag = None
            for k in range(w, energies):
                a, b = gl_all[k, 0, rows], gl_all[k, 1, rows]
                x, y = gg_all[k - w, 0, rows], gg_all[k - w, 1, rows]
                s, t = a * x - b * y, a * y + b * x
                real, imag = (s, t) if real is None else (real + s, imag + t)
            res[w, 0, rows] = real * scale
            res[w, 1, rows] = imag * scale
            return carry

        lax.fori_loop(0, share // 8, step, 0)

        @pl.when(w != e)
        def _():
            out_copy(w, e).start()

    keep = pltpu.make_async_copy(res.at[e], pol.at[e], local.at[0])
    keep.start()

    @pl.when(has_behind)
    def _():
        for k in range(3):
            hops[k].wait_recv()
            if k < 2:
                shared[2 + k].start()

    def hand_on(q):
        rows_out[0][q].wait_recv()

        @pl.when(has_onward)
        def _():
            rows_out[1][q].start()

    keep.wait()
    for q in range(energies):

        @pl.when(q != e)
        def _():
            out_copy(q, q).wait_recv()

        rows = pl.ds(q * share, share)
        for k in (0, 1):
            diag[k, rows] = onsite[k, 0, rows] - pol[q, k]
        if rows_out is not None:
            rows_out[0][q].start()
            if q > 0:
                hand_on(q - 1)
    if rows_out is not None:
        hand_on(energies - 1)

    for k in range(2):
        shared[k].wait_recv()

    @pl.when(has_behind)
    def _():
        for k in range(2):
            shared[2 + k].wait()

    for k in range(2):
        shared[k].wait_send()
    for k in range(3):
        direct[k].wait_send()

        @pl.when(has_onward)
        def _():
            hops[k].wait_send()

    for q in range(energies):

        @pl.when(q != e)
        def _():
            in_copy(0, q, e).wait_send()
            in_copy(1, q, e).wait_send()
            out_copy(q, e).wait_send()


def front(g_lesser, g_greater, onsite, lower, upper, rhs):
    energies = lax.axis_size("energy")
    n, columns = onsite.shape[2], rhs.shape[-1]
    share = n // energies
    vmem = pl.BlockSpec(memory_space=pltpu.VMEM)
    f32 = jnp.float32
    dma = pltpu.SemaphoreType.DMA
    pieces = pltpu.VMEM((energies, 2, share, n), f32)
    return pl.pallas_call(
        front_kernel,
        name="front",
        out_shape=(
            jax.ShapeDtypeStruct((2, n, n), f32),
            jax.ShapeDtypeStruct((2, 2, 2, n, n), f32),
            jax.ShapeDtypeStruct((2, 2, n, columns), f32),
        ),
        in_specs=[vmem] * 6,
        out_specs=(vmem,) * 3,
        scratch_shapes=[
            pltpu.VMEM((2, 2, n, n), f32),
            pieces, pieces, pieces, pieces,
            dma((2, energies)), dma((2, energies)), dma((energies,)), dma((energies,)),
            dma((3,)), dma((3,)), dma((3,)), dma((3,)),
            dma((2, 2)), dma((2, 2)), dma((2,)),
        ],
        compiler_params=pltpu.CompilerParams(collective_id=0, has_side_effects=True),
    )(g_lesser, g_greater, onsite, lower, upper, rhs)


def halves(x):
    high = x.astype(jnp.bfloat16)
    return high, (x - high.astype(jnp.float32)).astype(jnp.bfloat16)


def factor(a):
    return halves(a[0]), halves(a[1]), halves(a[0] + a[1])


def three_pass(a, b):
    dot = lambda u, v: jnp.dot(u, v, preferred_element_type=jnp.float32)
    return dot(a[0], b[0]) + (dot(a[0], b[1]) + dot(a[1], b[0]))


def times(a, b):
    first, second, third = (three_pass(a[k], b[k]) for k in range(3))
    return first - second, third - first - second


def inverse_of(matrix):
    eye_rows = lax.broadcasted_iota(jnp.int32, matrix[0].shape, 0)
    eye_columns = lax.broadcasted_iota(jnp.int32, matrix[0].shape, 1)
    eye = jnp.where(eye_rows == eye_columns, 1.0, 0.0)
    scale = 1.0 / diagonal_guess
    b = eye - matrix[0] * scale, -matrix[1] * scale
    fb = factor(b)
    square = times(fb, fb)
    cube = times(fb, factor(square))
    return (eye + b[0] + square[0] + cube[0]) * scale, (b[1] + square[1] + cube[1]) * scale


def whole_kernel(
    gl, gg, onsite, lower, upper, rhs, out, diag, near_lu, near_s,
    lu, gl_all, gg_all, res, pol,
    in_send, in_recv, out_send, out_recv, lu_send, lu_recv, piece_send, piece_recv,
    mate_send, mate_recv, local,
    d, s, near_d, g, got, direct_send, direct_recv, hop_send, hop_recv, g_send, g_recv,
):
    i, count = lax.axis_index("block"), lax.axis_size("block")
    energies = lax.axis_size("energy")
    n, columns = d.shape[-1], s.shape[-1]
    p, stride = lax.rem(i, 2), count // 2
    side = 1 - p
    pair, onward, behind = i + 1 - 2 * p, i + 2 - 4 * p, i - 2 + 4 * p
    has_onward = jnp.logical_and(onward >= 0, onward < count)
    has_behind = jnp.logical_and(behind >= 0, behind < count)
    partner = lax.rem(i + stride, count)

    def remote(src, dst, send, recv, where):
        return pltpu.make_async_remote_copy(
            src_ref=src, dst_ref=dst, send_sem=send, recv_sem=recv, device_id={"block": where}, device_id_type=MESH
        )

    tile = n // energies
    direct, hops = [], []
    for k in range(energies):
        rows = pl.ds(k * tile, tile)
        direct.append(remote(diag.at[:, rows], near_d.at[p, :, rows], direct_send.at[k], direct_recv.at[k], pair))
        hops.append(
            remote(near_d.at[side, :, rows], near_d.at[p, :, rows], hop_send.at[k], hop_recv.at[k], onward)
        )
    front_kernel(
        gl, gg, onsite, lower, upper, rhs, diag, near_lu, near_s,
        lu, gl_all, gg_all, res, pol,
        in_send, in_recv, out_send, out_recv, lu_send, lu_recv, piece_send, piece_recv,
        mate_send, mate_recv, local, (direct, hops), partner,
    )
    d[...] = diag[...]
    s[...] = rhs[:, 0]

    def update(which, kept):
        t = factor(times(factor((lu[which, 0], lu[which, 1])), factor(inverse_of((near_d[which, 0], near_d[which, 1])))))
        v = times(t, factor((near_lu[which, 1 - which, 0], near_lu[which, 1 - which, 1])))
        r = times(t, factor((near_s[which, 0], near_s[which, 1])))
        for k in (0, 1):
            d[k] = d[k] - v[k]
            s[k] = s[k] - r[k]

        @pl.when(kept)
        def _():
            c = times(t, factor((near_lu[which, which, 0], near_lu[which, which, 1])))
            for k in (0, 1):
                lu[which, k] = -c[k]

    update(side, has_onward)

    @pl.when(has_behind)
    def _():
        for k in range(energies):
            hops[k].wait_recv()
        update(p, has_behind)

    live = jnp.where(i < stride, 1, 0)
    inv = factor(inverse_of((d[0], d[1])))
    chunks = n // columns
    swaps = [remote(g.at[k], got.at[k], g_send.at[k], g_recv.at[k], partner) for k in range(chunks + 1)]
    for k in range(chunks + 1):
        if k == chunks:
            right = s[0], s[1]
        else:
            right = tuple(lu[live, m, :, k * columns : (k + 1) * columns] for m in (0, 1))
        part = times(inv, factor(right))
        g[k, 0], g[k, 1] = part
        swaps[k].start()
    coupling = factor((lu[live, 0], lu[live, 1]))
    for k in range(chunks + 1):
        swaps[k].wait_recv()
        change = times(coupling, factor((got[k, 0], got[k, 1])))
        for m in (0, 1):
            if k == chunks:
                s[m] = s[m] - change[m]
            else:
                cols = slice(k * columns, (k + 1) * columns)
                d[m, :, cols] = d[m, :, cols] - change[m]

    rows = lax.broadcasted_iota(jnp.int32, (n, n), 0)
    eye = jnp.where(rows == lax.broadcasted_iota(jnp.int32, (n, n), 1), 1.0, 0.0)
    scale = 1.0 / diagonal_guess
    b = factor((eye - d[0] * scale, -d[1] * scale))
    source = s[0], s[1]
    value = source
    for _ in range(3):
        value = plus(source, times(b, factor(value)))
    out[0, 0], out[1, 0] = value[0] * scale, value[1] * scale
    for k in range(energies):
        direct[k].wait_send()

        @pl.when(has_onward)
        def _():
            hops[k].wait_send()

    for k in range(chunks + 1):
        swaps[k].wait_send()


def whole(g_lesser, g_greater, onsite, lower, upper, rhs):
    energies = lax.axis_size("energy")
    n, columns = onsite.shape[2], rhs.shape[-1]
    vmem = pl.BlockSpec(memory_space=pltpu.VMEM)
    f32 = jnp.float32
    dma = pltpu.SemaphoreType.DMA
    chunks = n // columns + 1
    pieces = pltpu.VMEM((energies, 2, n // energies, n), f32)
    return pl.pallas_call(
        whole_kernel,
        name="whole",
        out_shape=jax.ShapeDtypeStruct((2, 1, n, columns), f32),
        in_specs=[vmem] * 6,
        out_specs=vmem,
        scratch_shapes=[
            pltpu.VMEM((2, n, n), f32),
            pltpu.VMEM((2, 2, 2, n, n), f32),
            pltpu.VMEM((2, 2, n, columns), f32),
            pltpu.VMEM((2, 2, n, n), f32),
            pieces, pieces, pieces, pieces,
            dma((2, energies)), dma((2, energies)), dma((energies,)), dma((energies,)),
            dma((3,)), dma((3,)), dma((3,)), dma((3,)),
            dma((2, 2)), dma((2, 2)), dma((2,)),
            pltpu.VMEM((2, n, n), f32),
            pltpu.VMEM((2, n, columns), f32),
            pltpu.VMEM((2, 2, n, n), f32),
            pltpu.VMEM((chunks, 2, n, columns), f32),
            pltpu.VMEM((chunks, 2, n, columns), f32),
            dma((energies,)), dma((energies,)), dma((energies,)), dma((energies,)),
            dma((chunks,)), dma((chunks,)),
        ],
        compiler_params=pltpu.CompilerParams(collective_id=1, has_side_effects=True),
    )(g_lesser, g_greater, onsite, lower, upper, rhs)


def shifted(value, steps):
    count = lax.axis_size("block")
    leading, last = max(0, -steps), min(count, count - steps)
    pairs = [(k, k + steps) for k in range(leading, last)]
    return lax.ppermute(value, "block", pairs)


def shards(g_lesser, g_greater, onsite, lower, upper, rhs):
    index = lax.axis_index("block")
    count = lax.axis_size("block")
    levels = count.bit_length() - 1
    n = onsite.shape[-1]
    both = jnp.concatenate(
        [jnp.where(index > 0, lower, 0.0), jnp.where(index < count - 1, upper, 0.0)], axis=-1
    )
    if levels == 2:
        return whole(g_lesser, g_greater, onsite, lower, upper, rhs)
    diag, near_lu, near_s = front(g_lesser, g_greater, onsite, lower, upper, rhs)
    diag = parts(diag)
    first, final = index < 2, index >= count - 2
    low, up = cut(parts(both), 0, n), cut(parts(both), n, 2 * n)
    source = parts(rhs[:, 0])
    for depth in range(levels):
        stride = 1 << depth
        inv = inverse(diag)
        if depth == levels - 1:
            coupling = tuple(jnp.where(index < stride, up[k], low[k]) for k in (0, 1))
            sent = product(inv, wide(coupling, source))
            swap = [(k, k ^ stride) for k in range(count)]
            got = parts(lax.ppermute(jnp.stack(sent), "block", swap))
            change = product(coupling, got)
            diag = minus(diag, cut(change, 0, n))
            source = minus(source, cut(change, n, None))
        elif depth == 0:
            packed = jnp.stack(inv)
            inv_left, inv_right = parts(shifted(packed, 1)), parts(shifted(packed, -1))
            t, w = product(low, inv_left), product(up, inv_right)
            lu_l, lu_r = near_lu[0], near_lu[1]
            change = product(t, wide(parts(lu_l[0]), parts(lu_l[1]), parts(near_s[0])))
            other = product(w, wide(parts(lu_r[0]), parts(lu_r[1]), parts(near_s[1])))
            change = tuple(jnp.where(index > 0, v, 0.0) for v in change)
            other = tuple(jnp.where(index < count - 1, v, 0.0) for v in other)
            diag = minus(minus(diag, cut(change, n, 2 * n)), cut(other, 0, n))
            source = minus(minus(source, cut(change, 2 * n, None)), cut(other, 2 * n, None))
            low = tuple(jnp.where(first, 0.0, -v) for v in cut(change, 0, n))
            up = tuple(jnp.where(final, 0.0, -v) for v in cut(other, n, 2 * n))
        else:
            sent = jnp.stack(product(inv, wide(low, up, source)))
            left, right = parts(shifted(sent, stride)), parts(shifted(sent, -stride))
            change, other = product(low, left), product(up, right)
            diag = minus(minus(diag, cut(change, n, 2 * n)), cut(other, 0, n))
            source = minus(minus(source, cut(change, 2 * n, None)), cut(other, 2 * n, None))
            low = tuple(-v for v in cut(change, 0, n))
            up = tuple(-v for v in cut(other, n, 2 * n))
    return jnp.stack(solve(diag, source))[:, None]


def solution(mesh):
    placed = (
        P(None, "energy", "block", None),
        P(None, "energy", "block", None),
        P(None, "energy", "block", None),
        P(None, "block", None),
        P(None, "block", None),
        P(None, "energy", "block", None),
    )
    return jax.shard_map(
        shards,
        mesh=mesh,
        in_specs=placed,
        out_specs=P(None, "energy", "block", None),
        check_vma=False,
    )
```

```python
import math

import jax
import jax.numpy as jnp
from jax import lax
from jax.experimental import pallas as pl
from jax.experimental.pallas import tpu as pltpu
from jax.sharding import PartitionSpec as P

diagonal_guess = 5.0
MODE = lax.Precision.HIGH
MESH = pl.DeviceIdType.MESH


def real_product(a, b):
    return jnp.matmul(a, b, precision=MODE)


def product(a, b):
    ar, ai = a
    br, bi = b
    return (
        real_product(ar, br) - real_product(ai, bi),
        real_product(ar, bi) + real_product(ai, br),
    )


def parts(a):
    return a[0], a[1]


def plus(a, b):
    return a[0] + b[0], a[1] + b[1]


def minus(a, b):
    return a[0] - b[0], a[1] - b[1]


def wide(*pieces):
    return tuple(jnp.concatenate([p[k] for p in pieces], axis=-1) for k in (0, 1))


def cut(a, start, stop):
    return a[0][:, start:stop], a[1][:, start:stop]


def remainder(matrix):
    eye = jnp.eye(matrix[0].shape[-1], dtype=jnp.float32)
    return eye - matrix[0] * (1.0 / diagonal_guess), -matrix[1] * (1.0 / diagonal_guess)


def inverse(matrix):
    eye = jnp.eye(matrix[0].shape[-1], dtype=jnp.float32)
    b = remainder(matrix)
    square = product(b, b)
    cube = product(b, square)
    scale = 1.0 / diagonal_guess
    return (eye + b[0] + square[0] + cube[0]) * scale, (b[1] + square[1] + cube[1]) * scale


def solve(matrix, source):
    b = remainder(matrix)
    value = source
    for _ in range(3):
        value = plus(source, product(b, value))
    scale = 1.0 / diagonal_guess
    return value[0] * scale, value[1] * scale


def front_kernel(
    gl, gg, onsite, lower, upper, rhs, diag, near_lu, near_s,
    lu, gl_all, gg_all, res, pol,
    in_send, in_recv, out_send, out_recv, lu_send, lu_recv, hop_send, hop_recv,
    mate_send, mate_recv, local, rows_out=None, partner=None,
):
    e, i = lax.axis_index("energy"), lax.axis_index("block")
    energies, count = lax.axis_size("energy"), lax.axis_size("block")
    share = gl.shape[2] // energies
    c, p = lax.rem(e, 2), lax.rem(i, 2)
    mate, side = e + 1 - 2 * c, 1 - p
    pair, onward, behind = i + 1 - 2 * p, i + 2 - 4 * p, i - 2 + 4 * p
    has_onward = jnp.logical_and(onward >= 0, onward < count)
    has_behind = jnp.logical_and(behind >= 0, behind < count)

    fill = [pltpu.make_async_copy((lower, upper)[k], lu.at[k], local.at[k]) for k in (0, 1)]
    for copy in fill:
        copy.start()
    barrier = pltpu.get_barrier_semaphore()
    for k in range(1, energies):
        pl.semaphore_signal(barrier, inc=1, device_id={"energy": lax.rem(e + k, energies)}, device_id_type=MESH)
    pl.semaphore_signal(barrier, inc=1, device_id={"block": pair}, device_id_type=MESH)

    @pl.when(has_onward)
    def _():
        pl.semaphore_signal(barrier, inc=1, device_id={"block": onward}, device_id_type=MESH)

    @pl.when(has_behind)
    def _():
        pl.semaphore_signal(barrier, inc=1, device_id={"block": behind}, device_id_type=MESH)

    peers = energies
    if partner is not None:
        peers = energies + 1
        pl.semaphore_signal(barrier, inc=1, device_id={"block": partner}, device_id_type=MESH)
    pl.semaphore_wait(barrier, peers + has_onward.astype(jnp.int32) + has_behind.astype(jnp.int32))

    def remote(src, dst, send, recv, **where):
        return pltpu.make_async_remote_copy(
            src_ref=src, dst_ref=dst, send_sem=send, recv_sem=recv, device_id=where, device_id_type=MESH
        )

    part = share // 2

    def in_copy(h, k, q, source):
        src, dst = ((gl, gl_all), (gg, gg_all))[k]
        rows = src.at[:, 0, pl.ds(q * share + h * part, part), :]
        there = dst.at[source, :, pl.ds(h * part, part), :]
        return remote(rows, there, in_send.at[h, k, q], in_recv.at[h, k, source], energy=q)

    def out_copy(h, w, source):
        rows = pl.ds(h * part, part)
        return remote(
            res.at[w, :, rows, :], pol.at[source, :, rows, :], out_send.at[h, w], out_recv.at[h, source], energy=w
        )

    for copy in fill:
        copy.wait()
    for h in (0, 1):
        for k in (0, 1):
            for q in range(energies):

                @pl.when(q != e)
                def _():
                    in_copy(h, k, q, e).start()

    own = []
    for k, (src, dst) in enumerate(((gl, gl_all), (gg, gg_all))):
        rows = src.at[:, 0, pl.ds(pl.multiple_of(e * share, 8), share), :]
        own.append(pltpu.make_async_copy(rows, dst.at[e], local.at[k]))
        own[-1].start()

    mine = (lu.at[c, 0], lu.at[c, 1], rhs.at[:, 0])

    def slot(s, k):
        return near_s.at[s] if k == 2 else near_lu.at[s, c, k]

    direct = [remote(mine[k], slot(p, k), lu_send.at[k], lu_recv.at[k], block=pair) for k in range(3)]
    hops = [remote(slot(side, k), slot(p, k), hop_send.at[k], hop_recv.at[k], block=onward) for k in range(3)]
    for copy in direct:
        copy.start()
    shared = [
        remote(slot(s, k), slot(s, k), mate_send.at[j, k], mate_recv.at[j, k], energy=mate)
        for j, s in enumerate((side, p))
        for k in (0, 1)
    ]
    for k in range(3):
        direct[k].wait_recv()

        @pl.when(has_onward)
        def _():
            hops[k].start()

        if k < 2:
            shared[k].start()

    for copy in own:
        copy.wait()
    scale = 1.0 / math.sqrt(energies)
    for h in (0, 1):
        for k in (0, 1):
            for q in range(energies):

                @pl.when(q != e)
                def _():
                    in_copy(h, k, q, q).wait_recv()

        for w in range(energies):

            def step(row, carry, w=w, h=h):
                rows = pl.ds(pl.multiple_of(h * part + row * 8, 8), 8)
                real = imag = None
                for k in range(w, energies):
                    a, b = gl_all[k, 0, rows], gl_all[k, 1, rows]
                    x, y = gg_all[k - w, 0, rows], gg_all[k - w, 1, rows]
                    s, t = a * x - b * y, a * y + b * x
                    real, imag = (s, t) if real is None else (real + s, imag + t)
                res[w, 0, rows] = real * scale
                res[w, 1, rows] = imag * scale
                return carry

            lax.fori_loop(0, part // 8, step, 0)

            @pl.when(w != e)
            def _():
                out_copy(h, w, e).start()

    keep = pltpu.make_async_copy(res.at[e], pol.at[e], local.at[0])
    keep.start()

    @pl.when(has_behind)
    def _():
        for k in range(3):
            hops[k].wait_recv()
            if k < 2:
                shared[2 + k].start()

    def hand_on(q):
        rows_out[0][q].wait_recv()

        @pl.when(has_onward)
        def _():
            rows_out[1][q].start()

    keep.wait()
    for q in range(energies):

        @pl.when(q != e)
        def _():
            out_copy(0, q, q).wait_recv()
            out_copy(1, q, q).wait_recv()

        rows = pl.ds(q * share, share)
        for k in (0, 1):
            diag[k, rows] = onsite[k, 0, rows] - pol[q, k]
        if rows_out is not None:
            rows_out[0][q].start()
            if q > 0:
                hand_on(q - 1)
    if rows_out is not None:
        hand_on(energies - 1)

    for k in range(2):
        shared[k].wait_recv()

    @pl.when(has_behind)
    def _():
        for k in range(2):
            shared[2 + k].wait()

    for k in range(2):
        shared[k].wait_send()
    for k in range(3):
        direct[k].wait_send()

        @pl.when(has_onward)
        def _():
            hops[k].wait_send()

    for q in range(energies):

        @pl.when(q != e)
        def _():
            for h in (0, 1):
                in_copy(h, 0, q, e).wait_send()
                in_copy(h, 1, q, e).wait_send()
                out_copy(h, q, e).wait_send()


def front(g_lesser, g_greater, onsite, lower, upper, rhs):
    energies = lax.axis_size("energy")
    n, columns = onsite.shape[2], rhs.shape[-1]
    share = n // energies
    vmem = pl.BlockSpec(memory_space=pltpu.VMEM)
    f32 = jnp.float32
    dma = pltpu.SemaphoreType.DMA
    pieces = pltpu.VMEM((energies, 2, share, n), f32)
    return pl.pallas_call(
        front_kernel,
        name="front",
        out_shape=(
            jax.ShapeDtypeStruct((2, n, n), f32),
            jax.ShapeDtypeStruct((2, 2, 2, n, n), f32),
            jax.ShapeDtypeStruct((2, 2, n, columns), f32),
        ),
        in_specs=[vmem] * 6,
        out_specs=(vmem,) * 3,
        scratch_shapes=[
            pltpu.VMEM((2, 2, n, n), f32),
            pieces, pieces, pieces, pieces,
            dma((2, 2, energies)), dma((2, 2, energies)), dma((2, energies)), dma((2, energies)),
            dma((3,)), dma((3,)), dma((3,)), dma((3,)),
            dma((2, 2)), dma((2, 2)), dma((2,)),
        ],
        compiler_params=pltpu.CompilerParams(collective_id=0, has_side_effects=True),
    )(g_lesser, g_greater, onsite, lower, upper, rhs)


def halves(x):
    high = x.astype(jnp.bfloat16)
    return high, (x - high.astype(jnp.float32)).astype(jnp.bfloat16)


def factor(a):
    return halves(a[0]), halves(a[1]), halves(a[0] + a[1])


def three_pass(a, b):
    dot = lambda u, v: jnp.dot(u, v, preferred_element_type=jnp.float32)
    return dot(a[0], b[0]) + (dot(a[0], b[1]) + dot(a[1], b[0]))


def times(a, b):
    first, second, third = (three_pass(a[k], b[k]) for k in range(3))
    return first - second, third - first - second


def inverse_of(matrix):
    eye_rows = lax.broadcasted_iota(jnp.int32, matrix[0].shape, 0)
    eye_columns = lax.broadcasted_iota(jnp.int32, matrix[0].shape, 1)
    eye = jnp.where(eye_rows == eye_columns, 1.0, 0.0)
    scale = 1.0 / diagonal_guess
    b = eye - matrix[0] * scale, -matrix[1] * scale
    fb = factor(b)
    square = times(fb, fb)
    cube = times(fb, factor(square))
    return (eye + b[0] + square[0] + cube[0]) * scale, (b[1] + square[1] + cube[1]) * scale


def whole_kernel(
    gl, gg, onsite, lower, upper, rhs, out, diag, near_lu, near_s,
    lu, gl_all, gg_all, res, pol,
    in_send, in_recv, out_send, out_recv, lu_send, lu_recv, piece_send, piece_recv,
    mate_send, mate_recv, local,
    d, s, near_d, g, got, direct_send, direct_recv, hop_send, hop_recv, g_send, g_recv,
):
    i, count = lax.axis_index("block"), lax.axis_size("block")
    energies = lax.axis_size("energy")
    n, columns = d.shape[-1], s.shape[-1]
    p, stride = lax.rem(i, 2), count // 2
    side = 1 - p
    pair, onward, behind = i + 1 - 2 * p, i + 2 - 4 * p, i - 2 + 4 * p
    has_onward = jnp.logical_and(onward >= 0, onward < count)
    has_behind = jnp.logical_and(behind >= 0, behind < count)
    partner = lax.rem(i + stride, count)

    def remote(src, dst, send, recv, where):
        return pltpu.make_async_remote_copy(
            src_ref=src, dst_ref=dst, send_sem=send, recv_sem=recv, device_id={"block": where}, device_id_type=MESH
        )

    tile = n // energies
    direct, hops = [], []
    for k in range(energies):
        rows = pl.ds(k * tile, tile)
        direct.append(remote(diag.at[:, rows], near_d.at[p, :, rows], direct_send.at[k], direct_recv.at[k], pair))
        hops.append(
            remote(near_d.at[side, :, rows], near_d.at[p, :, rows], hop_send.at[k], hop_recv.at[k], onward)
        )
    front_kernel(
        gl, gg, onsite, lower, upper, rhs, diag, near_lu, near_s,
        lu, gl_all, gg_all, res, pol,
        in_send, in_recv, out_send, out_recv, lu_send, lu_recv, piece_send, piece_recv,
        mate_send, mate_recv, local, (direct, hops), partner,
    )
    d[...] = diag[...]
    s[...] = rhs[:, 0]

    def update(which, kept):
        t = factor(times(factor((lu[which, 0], lu[which, 1])), factor(inverse_of((near_d[which, 0], near_d[which, 1])))))
        v = times(t, factor((near_lu[which, 1 - which, 0], near_lu[which, 1 - which, 1])))
        r = times(t, factor((near_s[which, 0], near_s[which, 1])))
        for k in (0, 1):
            d[k] = d[k] - v[k]
            s[k] = s[k] - r[k]

        @pl.when(kept)
        def _():
            c = times(t, factor((near_lu[which, which, 0], near_lu[which, which, 1])))
            for k in (0, 1):
                lu[which, k] = -c[k]

    update(side, has_onward)

    @pl.when(has_behind)
    def _():
        for k in range(energies):
            hops[k].wait_recv()
        update(p, has_behind)

    live = jnp.where(i < stride, 1, 0)
    inv = factor(inverse_of((d[0], d[1])))
    chunks = n // columns
    swaps = [remote(g.at[k], got.at[k], g_send.at[k], g_recv.at[k], partner) for k in range(chunks + 1)]
    for k in range(chunks + 1):
        if k == chunks:
            right = s[0], s[1]
        else:
            right = tuple(lu[live, m, :, k * columns : (k + 1) * columns] for m in (0, 1))
        part = times(inv, factor(right))
        g[k, 0], g[k, 1] = part
        swaps[k].start()
    coupling = factor((lu[live, 0], lu[live, 1]))
    for k in range(chunks + 1):
        swaps[k].wait_recv()
        change = times(coupling, factor((got[k, 0], got[k, 1])))
        for m in (0, 1):
            if k == chunks:
                s[m] = s[m] - change[m]
            else:
                cols = slice(k * columns, (k + 1) * columns)
                d[m, :, cols] = d[m, :, cols] - change[m]

    rows = lax.broadcasted_iota(jnp.int32, (n, n), 0)
    eye = jnp.where(rows == lax.broadcasted_iota(jnp.int32, (n, n), 1), 1.0, 0.0)
    scale = 1.0 / diagonal_guess
    b = factor((eye - d[0] * scale, -d[1] * scale))
    source = s[0], s[1]
    value = source
    for _ in range(3):
        value = plus(source, times(b, factor(value)))
    out[0, 0], out[1, 0] = value[0] * scale, value[1] * scale
    for k in range(energies):
        direct[k].wait_send()

        @pl.when(has_onward)
        def _():
            hops[k].wait_send()

    for k in range(chunks + 1):
        swaps[k].wait_send()


def whole(g_lesser, g_greater, onsite, lower, upper, rhs):
    energies = lax.axis_size("energy")
    n, columns = onsite.shape[2], rhs.shape[-1]
    vmem = pl.BlockSpec(memory_space=pltpu.VMEM)
    f32 = jnp.float32
    dma = pltpu.SemaphoreType.DMA
    chunks = n // columns + 1
    pieces = pltpu.VMEM((energies, 2, n // energies, n), f32)
    return pl.pallas_call(
        whole_kernel,
        name="whole",
        out_shape=jax.ShapeDtypeStruct((2, 1, n, columns), f32),
        in_specs=[vmem] * 6,
        out_specs=vmem,
        scratch_shapes=[
            pltpu.VMEM((2, n, n), f32),
            pltpu.VMEM((2, 2, 2, n, n), f32),
            pltpu.VMEM((2, 2, n, columns), f32),
            pltpu.VMEM((2, 2, n, n), f32),
            pieces, pieces, pieces, pieces,
            dma((2, 2, energies)), dma((2, 2, energies)), dma((2, energies)), dma((2, energies)),
            dma((3,)), dma((3,)), dma((3,)), dma((3,)),
            dma((2, 2)), dma((2, 2)), dma((2,)),
            pltpu.VMEM((2, n, n), f32),
            pltpu.VMEM((2, n, columns), f32),
            pltpu.VMEM((2, 2, n, n), f32),
            pltpu.VMEM((chunks, 2, n, columns), f32),
            pltpu.VMEM((chunks, 2, n, columns), f32),
            dma((energies,)), dma((energies,)), dma((energies,)), dma((energies,)),
            dma((chunks,)), dma((chunks,)),
        ],
        compiler_params=pltpu.CompilerParams(collective_id=1, has_side_effects=True),
    )(g_lesser, g_greater, onsite, lower, upper, rhs)


def shifted(value, steps):
    count = lax.axis_size("block")
    leading, last = max(0, -steps), min(count, count - steps)
    pairs = [(k, k + steps) for k in range(leading, last)]
    return lax.ppermute(value, "block", pairs)


def shards(g_lesser, g_greater, onsite, lower, upper, rhs):
    index = lax.axis_index("block")
    count = lax.axis_size("block")
    levels = count.bit_length() - 1
    n = onsite.shape[-1]
    both = jnp.concatenate(
        [jnp.where(index > 0, lower, 0.0), jnp.where(index < count - 1, upper, 0.0)], axis=-1
    )
    if levels == 2:
        return whole(g_lesser, g_greater, onsite, lower, upper, rhs)
    diag, near_lu, near_s = front(g_lesser, g_greater, onsite, lower, upper, rhs)
    diag = parts(diag)
    first, final = index < 2, index >= count - 2
    low, up = cut(parts(both), 0, n), cut(parts(both), n, 2 * n)
    source = parts(rhs[:, 0])
    for depth in range(levels):
        stride = 1 << depth
        inv = inverse(diag)
        if depth == levels - 1:
            coupling = tuple(jnp.where(index < stride, up[k], low[k]) for k in (0, 1))
            sent = product(inv, wide(coupling, source))
            swap = [(k, k ^ stride) for k in range(count)]
            got = parts(lax.ppermute(jnp.stack(sent), "block", swap))
            change = product(coupling, got)
            diag = minus(diag, cut(change, 0, n))
            source = minus(source, cut(change, n, None))
        elif depth == 0:
            packed = jnp.stack(inv)
            inv_left, inv_right = parts(shifted(packed, 1)), parts(shifted(packed, -1))
            t, w = product(low, inv_left), product(up, inv_right)
            lu_l, lu_r = near_lu[0], near_lu[1]
            change = product(t, wide(parts(lu_l[0]), parts(lu_l[1]), parts(near_s[0])))
            other = product(w, wide(parts(lu_r[0]), parts(lu_r[1]), parts(near_s[1])))
            change = tuple(jnp.where(index > 0, v, 0.0) for v in change)
            other = tuple(jnp.where(index < count - 1, v, 0.0) for v in other)
            diag = minus(minus(diag, cut(change, n, 2 * n)), cut(other, 0, n))
            source = minus(minus(source, cut(change, 2 * n, None)), cut(other, 2 * n, None))
            low = tuple(jnp.where(first, 0.0, -v) for v in cut(change, 0, n))
            up = tuple(jnp.where(final, 0.0, -v) for v in cut(other, n, 2 * n))
        else:
            sent = jnp.stack(product(inv, wide(low, up, source)))
            left, right = parts(shifted(sent, stride)), parts(shifted(sent, -stride))
            change, other = product(low, left), product(up, right)
            diag = minus(minus(diag, cut(change, n, 2 * n)), cut(other, 0, n))
            source = minus(minus(source, cut(change, 2 * n, None)), cut(other, 2 * n, None))
            low = tuple(-v for v in cut(change, 0, n))
            up = tuple(-v for v in cut(other, n, 2 * n))
    return jnp.stack(solve(diag, source))[:, None]


def solution(mesh):
    placed = (
        P(None, "energy", "block", None),
        P(None, "energy", "block", None),
        P(None, "energy", "block", None),
        P(None, "block", None),
        P(None, "block", None),
        P(None, "energy", "block", None),
    )
    return jax.shard_map(
        shards,
        mesh=mesh,
        in_specs=placed,
        out_specs=P(None, "energy", "block", None),
        check_vma=False,
    )
```

```python
import math

import jax
import jax.numpy as jnp
from jax import lax
from jax.experimental import pallas as pl
from jax.experimental.pallas import tpu as pltpu
from jax.sharding import PartitionSpec as P

diagonal_guess = 5.0
MODE = lax.Precision.HIGH
MESH = pl.DeviceIdType.MESH


def real_product(a, b):
    return jnp.matmul(a, b, precision=MODE)


def product(a, b):
    ar, ai = a
    br, bi = b
    return (
        real_product(ar, br) - real_product(ai, bi),
        real_product(ar, bi) + real_product(ai, br),
    )


def parts(a):
    return a[0], a[1]


def plus(a, b):
    return a[0] + b[0], a[1] + b[1]


def minus(a, b):
    return a[0] - b[0], a[1] - b[1]


def wide(*pieces):
    return tuple(jnp.concatenate([p[k] for p in pieces], axis=-1) for k in (0, 1))


def cut(a, start, stop):
    return a[0][:, start:stop], a[1][:, start:stop]


def remainder(matrix):
    eye = jnp.eye(matrix[0].shape[-1], dtype=jnp.float32)
    return eye - matrix[0] * (1.0 / diagonal_guess), -matrix[1] * (1.0 / diagonal_guess)


def inverse(matrix):
    eye = jnp.eye(matrix[0].shape[-1], dtype=jnp.float32)
    b = remainder(matrix)
    square = product(b, b)
    cube = product(b, square)
    scale = 1.0 / diagonal_guess
    return (eye + b[0] + square[0] + cube[0]) * scale, (b[1] + square[1] + cube[1]) * scale


def solve(matrix, source):
    b = remainder(matrix)
    value = source
    for _ in range(3):
        value = plus(source, product(b, value))
    scale = 1.0 / diagonal_guess
    return value[0] * scale, value[1] * scale


def front_kernel(
    gl, gg, onsite, lower, upper, rhs, diag, near_lu, near_s,
    lu, gl_all, gg_all, res, pol,
    in_send, in_recv, out_send, out_recv, lu_send, lu_recv, hop_send, hop_recv,
    mate_send, mate_recv, local, rows_out=None, partner=None,
):
    e, i = lax.axis_index("energy"), lax.axis_index("block")
    energies, count = lax.axis_size("energy"), lax.axis_size("block")
    share = gl.shape[2] // energies
    c, p = lax.rem(e, 2), lax.rem(i, 2)
    mate, side = e + 1 - 2 * c, 1 - p
    pair, onward, behind = i + 1 - 2 * p, i + 2 - 4 * p, i - 2 + 4 * p
    has_onward = jnp.logical_and(onward >= 0, onward < count)
    has_behind = jnp.logical_and(behind >= 0, behind < count)

    fill = [pltpu.make_async_copy((lower, upper)[k], lu.at[k], local.at[k]) for k in (0, 1)]
    for copy in fill:
        copy.start()
    barrier = pltpu.get_barrier_semaphore()
    for k in range(1, energies):
        pl.semaphore_signal(barrier, inc=1, device_id={"energy": lax.rem(e + k, energies)}, device_id_type=MESH)
    pl.semaphore_signal(barrier, inc=1, device_id={"block": pair}, device_id_type=MESH)

    @pl.when(has_onward)
    def _():
        pl.semaphore_signal(barrier, inc=1, device_id={"block": onward}, device_id_type=MESH)

    @pl.when(has_behind)
    def _():
        pl.semaphore_signal(barrier, inc=1, device_id={"block": behind}, device_id_type=MESH)

    peers = energies
    if partner is not None:
        peers = energies + 1
        pl.semaphore_signal(barrier, inc=1, device_id={"block": partner}, device_id_type=MESH)
    pl.semaphore_wait(barrier, peers + has_onward.astype(jnp.int32) + has_behind.astype(jnp.int32))

    def remote(src, dst, send, recv, **where):
        return pltpu.make_async_remote_copy(
            src_ref=src, dst_ref=dst, send_sem=send, recv_sem=recv, device_id=where, device_id_type=MESH
        )

    part = share // 2

    def in_copy(h, k, q, source):
        src, dst = ((gl, gl_all), (gg, gg_all))[k]
        rows = src.at[:, 0, pl.ds(q * share + h * part, part), :]
        there = dst.at[source, :, pl.ds(h * part, part), :]
        return remote(rows, there, in_send.at[h, k, q], in_recv.at[h, k, source], energy=q)

    def out_copy(h, w, source):
        rows = pl.ds(h * part, part)
        return remote(
            res.at[w, :, rows, :], pol.at[source, :, rows, :], out_send.at[h, w], out_recv.at[h, source], energy=w
        )

    for copy in fill:
        copy.wait()
    for h in (0, 1):
        for k in (0, 1):
            for q in range(energies):

                @pl.when(q != e)
                def _():
                    in_copy(h, k, q, e).start()

    own = []
    for k, (src, dst) in enumerate(((gl, gl_all), (gg, gg_all))):
        rows = src.at[:, 0, pl.ds(pl.multiple_of(e * share, 8), share), :]
        own.append(pltpu.make_async_copy(rows, dst.at[e], local.at[k]))
        own[-1].start()

    mine = (lu.at[c, 0], lu.at[c, 1], rhs.at[:, 0])

    def slot(s, k):
        return near_s.at[s] if k == 2 else near_lu.at[s, c, k]

    direct = [remote(mine[k], slot(p, k), lu_send.at[k], lu_recv.at[k], block=pair) for k in range(3)]
    hops = [remote(slot(side, k), slot(p, k), hop_send.at[k], hop_recv.at[k], block=onward) for k in range(3)]
    for copy in direct:
        copy.start()
    shared = [
        remote(slot(s, k), slot(s, k), mate_send.at[j, k], mate_recv.at[j, k], energy=mate)
        for j, s in enumerate((side, p))
        for k in (0, 1)
    ]
    for k in range(3):
        direct[k].wait_recv()

        @pl.when(has_onward)
        def _():
            hops[k].start()

        if k < 2:
            shared[k].start()

    for copy in own:
        copy.wait()
    scale = 1.0 / math.sqrt(energies)
    for h in (0, 1):
        for k in (0, 1):
            for q in range(energies):

                @pl.when(q != e)
                def _():
                    in_copy(h, k, q, q).wait_recv()

        for w in range(energies):

            def step(row, carry, w=w, h=h):
                rows = pl.ds(pl.multiple_of(h * part + row * 8, 8), 8)
                real = imag = None
                for k in range(w, energies):
                    a, b = gl_all[k, 0, rows], gl_all[k, 1, rows]
                    x, y = gg_all[k - w, 0, rows], gg_all[k - w, 1, rows]
                    s, t = a * x - b * y, a * y + b * x
                    real, imag = (s, t) if real is None else (real + s, imag + t)
                res[w, 0, rows] = real * scale
                res[w, 1, rows] = imag * scale
                return carry

            lax.fori_loop(0, part // 8, step, 0)

            @pl.when(w != e)
            def _():
                out_copy(h, w, e).start()

    keep = pltpu.make_async_copy(res.at[e], pol.at[e], local.at[0])
    keep.start()

    @pl.when(has_behind)
    def _():
        for k in range(3):
            hops[k].wait_recv()
            if k < 2:
                shared[2 + k].start()

    def hand_on(q):
        rows_out[0][q].wait_recv()

        @pl.when(has_onward)
        def _():
            rows_out[1][q].start()

    keep.wait()
    for q in range(energies):

        @pl.when(q != e)
        def _():
            out_copy(0, q, q).wait_recv()
            out_copy(1, q, q).wait_recv()

        rows = pl.ds(q * share, share)
        for k in (0, 1):
            diag[k, rows] = onsite[k, 0, rows] - pol[q, k]
        if rows_out is not None:
            rows_out[0][q].start()
            if q > 0:
                hand_on(q - 1)
    if rows_out is not None:
        hand_on(energies - 1)

    for k in range(2):
        shared[k].wait_recv()

    @pl.when(has_behind)
    def _():
        for k in range(2):
            shared[2 + k].wait()

    for k in range(2):
        shared[k].wait_send()
    for k in range(3):
        direct[k].wait_send()

        @pl.when(has_onward)
        def _():
            hops[k].wait_send()

    for q in range(energies):

        @pl.when(q != e)
        def _():
            for h in (0, 1):
                in_copy(h, 0, q, e).wait_send()
                in_copy(h, 1, q, e).wait_send()
                out_copy(h, q, e).wait_send()


def front(g_lesser, g_greater, onsite, lower, upper, rhs):
    energies = lax.axis_size("energy")
    n, columns = onsite.shape[2], rhs.shape[-1]
    share = n // energies
    vmem = pl.BlockSpec(memory_space=pltpu.VMEM)
    f32 = jnp.float32
    dma = pltpu.SemaphoreType.DMA
    pieces = pltpu.VMEM((energies, 2, share, n), f32)
    return pl.pallas_call(
        front_kernel,
        name="front",
        out_shape=(
            jax.ShapeDtypeStruct((2, n, n), f32),
            jax.ShapeDtypeStruct((2, 2, 2, n, n), f32),
            jax.ShapeDtypeStruct((2, 2, n, columns), f32),
        ),
        in_specs=[vmem] * 6,
        out_specs=(vmem,) * 3,
        scratch_shapes=[
            pltpu.VMEM((2, 2, n, n), f32),
            pieces, pieces, pieces, pieces,
            dma((2, 2, energies)), dma((2, 2, energies)), dma((2, energies)), dma((2, energies)),
            dma((3,)), dma((3,)), dma((3,)), dma((3,)),
            dma((2, 2)), dma((2, 2)), dma((2,)),
        ],
        compiler_params=pltpu.CompilerParams(collective_id=0, has_side_effects=True),
    )(g_lesser, g_greater, onsite, lower, upper, rhs)


def halves(x):
    high = x.astype(jnp.bfloat16)
    return high, (x - high.astype(jnp.float32)).astype(jnp.bfloat16)


def factor(a):
    return halves(a[0]), halves(a[1]), halves(a[0] + a[1])


def three_pass(a, b):
    dot = lambda u, v: jnp.dot(u, v, preferred_element_type=jnp.float32)
    return dot(a[0], b[0]) + (dot(a[0], b[1]) + dot(a[1], b[0]))


def times(a, b):
    first, second, third = (three_pass(a[k], b[k]) for k in range(3))
    return first - second, third - first - second


def inverse_of(matrix):
    eye_rows = lax.broadcasted_iota(jnp.int32, matrix[0].shape, 0)
    eye_columns = lax.broadcasted_iota(jnp.int32, matrix[0].shape, 1)
    eye = jnp.where(eye_rows == eye_columns, 1.0, 0.0)
    scale = 1.0 / diagonal_guess
    b = eye - matrix[0] * scale, -matrix[1] * scale
    fb = factor(b)
    square = times(fb, fb)
    cube = times(fb, factor(square))
    return (eye + b[0] + square[0] + cube[0]) * scale, (b[1] + square[1] + cube[1]) * scale


def whole_kernel(
    gl, gg, onsite, lower, upper, rhs, out, diag, near_lu, near_s,
    lu, gl_all, gg_all, res, pol,
    in_send, in_recv, out_send, out_recv, lu_send, lu_recv, piece_send, piece_recv,
    mate_send, mate_recv, local,
    d, s, near_d, g, got, direct_send, direct_recv, hop_send, hop_recv, g_send, g_recv,
):
    i, count = lax.axis_index("block"), lax.axis_size("block")
    energies = lax.axis_size("energy")
    n, columns = d.shape[-1], s.shape[-1]
    p, stride = lax.rem(i, 2), count // 2
    side = 1 - p
    pair, onward, behind = i + 1 - 2 * p, i + 2 - 4 * p, i - 2 + 4 * p
    has_onward = jnp.logical_and(onward >= 0, onward < count)
    has_behind = jnp.logical_and(behind >= 0, behind < count)
    partner = lax.rem(i + stride, count)

    def remote(src, dst, send, recv, where):
        return pltpu.make_async_remote_copy(
            src_ref=src, dst_ref=dst, send_sem=send, recv_sem=recv, device_id={"block": where}, device_id_type=MESH
        )

    tile = n // energies
    direct, hops = [], []
    for k in range(energies):
        rows = pl.ds(k * tile, tile)
        direct.append(remote(diag.at[:, rows], near_d.at[p, :, rows], direct_send.at[k], direct_recv.at[k], pair))
        hops.append(
            remote(near_d.at[side, :, rows], near_d.at[p, :, rows], hop_send.at[k], hop_recv.at[k], onward)
        )
    front_kernel(
        gl, gg, onsite, lower, upper, rhs, diag, near_lu, near_s,
        lu, gl_all, gg_all, res, pol,
        in_send, in_recv, out_send, out_recv, lu_send, lu_recv, piece_send, piece_recv,
        mate_send, mate_recv, local, (direct, hops), partner,
    )
    d[...] = diag[...]
    s[...] = rhs[:, 0]

    def update(which, kept):
        t = factor(times(factor((lu[which, 0], lu[which, 1])), factor(inverse_of((near_d[which, 0], near_d[which, 1])))))
        v = times(t, factor((near_lu[which, 1 - which, 0], near_lu[which, 1 - which, 1])))
        r = times(t, factor((near_s[which, 0], near_s[which, 1])))
        for k in (0, 1):
            d[k] = d[k] - v[k]
            s[k] = s[k] - r[k]

        @pl.when(kept)
        def _():
            c = times(t, factor((near_lu[which, which, 0], near_lu[which, which, 1])))
            for k in (0, 1):
                lu[which, k] = -c[k]

    update(side, has_onward)

    @pl.when(has_behind)
    def _():
        for k in range(energies):
            hops[k].wait_recv()
        update(p, has_behind)

    live = jnp.where(i < stride, 1, 0)
    inv = factor(inverse_of((d[0], d[1])))
    chunks = n // columns
    swaps = [remote(g.at[k], got.at[k], g_send.at[k], g_recv.at[k], partner) for k in range(chunks + 1)]
    for k in range(chunks + 1):
        if k == chunks:
            right = s[0], s[1]
        else:
            right = tuple(lu[live, m, :, k * columns : (k + 1) * columns] for m in (0, 1))
        part = times(inv, factor(right))
        g[k, 0], g[k, 1] = part
        swaps[k].start()
    coupling = factor((lu[live, 0], lu[live, 1]))
    for k in range(chunks):
        swaps[k].wait_recv()
        change = times(coupling, factor((got[k, 0], got[k, 1])))
        cols = slice(k * columns, (k + 1) * columns)
        for m in (0, 1):
            d[m, :, cols] = d[m, :, cols] - change[m]
    final = factor(inverse_of((d[0], d[1])))
    swaps[chunks].wait_recv()
    change = times(coupling, factor((got[chunks, 0], got[chunks, 1])))
    value = times(final, factor((s[0] - change[0], s[1] - change[1])))
    out[0, 0], out[1, 0] = value
    for k in range(energies):
        direct[k].wait_send()

        @pl.when(has_onward)
        def _():
            hops[k].wait_send()

    for k in range(chunks + 1):
        swaps[k].wait_send()


def whole(g_lesser, g_greater, onsite, lower, upper, rhs):
    energies = lax.axis_size("energy")
    n, columns = onsite.shape[2], rhs.shape[-1]
    vmem = pl.BlockSpec(memory_space=pltpu.VMEM)
    f32 = jnp.float32
    dma = pltpu.SemaphoreType.DMA
    chunks = n // columns + 1
    pieces = pltpu.VMEM((energies, 2, n // energies, n), f32)
    return pl.pallas_call(
        whole_kernel,
        name="whole",
        out_shape=jax.ShapeDtypeStruct((2, 1, n, columns), f32),
        in_specs=[vmem] * 6,
        out_specs=vmem,
        scratch_shapes=[
            pltpu.VMEM((2, n, n), f32),
            pltpu.VMEM((2, 2, 2, n, n), f32),
            pltpu.VMEM((2, 2, n, columns), f32),
            pltpu.VMEM((2, 2, n, n), f32),
            pieces, pieces, pieces, pieces,
            dma((2, 2, energies)), dma((2, 2, energies)), dma((2, energies)), dma((2, energies)),
            dma((3,)), dma((3,)), dma((3,)), dma((3,)),
            dma((2, 2)), dma((2, 2)), dma((2,)),
            pltpu.VMEM((2, n, n), f32),
            pltpu.VMEM((2, n, columns), f32),
            pltpu.VMEM((2, 2, n, n), f32),
            pltpu.VMEM((chunks, 2, n, columns), f32),
            pltpu.VMEM((chunks, 2, n, columns), f32),
            dma((energies,)), dma((energies,)), dma((energies,)), dma((energies,)),
            dma((chunks,)), dma((chunks,)),
        ],
        compiler_params=pltpu.CompilerParams(collective_id=1, has_side_effects=True),
    )(g_lesser, g_greater, onsite, lower, upper, rhs)


def shifted(value, steps):
    count = lax.axis_size("block")
    leading, last = max(0, -steps), min(count, count - steps)
    pairs = [(k, k + steps) for k in range(leading, last)]
    return lax.ppermute(value, "block", pairs)


def shards(g_lesser, g_greater, onsite, lower, upper, rhs):
    index = lax.axis_index("block")
    count = lax.axis_size("block")
    levels = count.bit_length() - 1
    n = onsite.shape[-1]
    both = jnp.concatenate(
        [jnp.where(index > 0, lower, 0.0), jnp.where(index < count - 1, upper, 0.0)], axis=-1
    )
    if levels == 2:
        return whole(g_lesser, g_greater, onsite, lower, upper, rhs)
    diag, near_lu, near_s = front(g_lesser, g_greater, onsite, lower, upper, rhs)
    diag = parts(diag)
    first, final = index < 2, index >= count - 2
    low, up = cut(parts(both), 0, n), cut(parts(both), n, 2 * n)
    source = parts(rhs[:, 0])
    for depth in range(levels):
        stride = 1 << depth
        inv = inverse(diag)
        if depth == levels - 1:
            coupling = tuple(jnp.where(index < stride, up[k], low[k]) for k in (0, 1))
            sent = product(inv, wide(coupling, source))
            swap = [(k, k ^ stride) for k in range(count)]
            got = parts(lax.ppermute(jnp.stack(sent), "block", swap))
            change = product(coupling, got)
            diag = minus(diag, cut(change, 0, n))
            source = minus(source, cut(change, n, None))
        elif depth == 0:
            packed = jnp.stack(inv)
            inv_left, inv_right = parts(shifted(packed, 1)), parts(shifted(packed, -1))
            t, w = product(low, inv_left), product(up, inv_right)
            lu_l, lu_r = near_lu[0], near_lu[1]
            change = product(t, wide(parts(lu_l[0]), parts(lu_l[1]), parts(near_s[0])))
            other = product(w, wide(parts(lu_r[0]), parts(lu_r[1]), parts(near_s[1])))
            change = tuple(jnp.where(index > 0, v, 0.0) for v in change)
            other = tuple(jnp.where(index < count - 1, v, 0.0) for v in other)
            diag = minus(minus(diag, cut(change, n, 2 * n)), cut(other, 0, n))
            source = minus(minus(source, cut(change, 2 * n, None)), cut(other, 2 * n, None))
            low = tuple(jnp.where(first, 0.0, -v) for v in cut(change, 0, n))
            up = tuple(jnp.where(final, 0.0, -v) for v in cut(other, n, 2 * n))
        else:
            sent = jnp.stack(product(inv, wide(low, up, source)))
            left, right = parts(shifted(sent, stride)), parts(shifted(sent, -stride))
            change, other = product(low, left), product(up, right)
            diag = minus(minus(diag, cut(change, n, 2 * n)), cut(other, 0, n))
            source = minus(minus(source, cut(change, 2 * n, None)), cut(other, 2 * n, None))
            low = tuple(-v for v in cut(change, 0, n))
            up = tuple(-v for v in cut(other, n, 2 * n))
    return jnp.stack(solve(diag, source))[:, None]


def solution(mesh):
    placed = (
        P(None, "energy", "block", None),
        P(None, "energy", "block", None),
        P(None, "energy", "block", None),
        P(None, "block", None),
        P(None, "block", None),
        P(None, "energy", "block", None),
    )
    return jax.shard_map(
        shards,
        mesh=mesh,
        in_specs=placed,
        out_specs=P(None, "energy", "block", None),
        check_vma=False,
    )
```
